32 devices in a mesh: grp: 4 (over y, core), dev: 8 (over z, x).
Axes of the slice: x: 2, y: 2, z: 4, core: 2. Of those that a mesh axis runs over, the one named last changes fastest.
Arguments:
- samples: int32 [128, 515, 1024], P(('grp', 'dev')), may hold values from -128 to 127
- taps: int32 [4, 1024], replicated, may hold values from -1024 to 1024
Outputs:
- gram: float32 [2, 512, 128, 128], P(None, ('grp', 'dev'))
The draws below stay inside these ranges and needn't reach their ends.
All inputs are finite; a program needn't handle non-finite values.
Results may differ from the reference program's by a relative error of at most 0.0029.
Values may be sent and summed in bfloat16 or wider, within the bound.
No kernel may reach another device: no remote copies, remote signals or barrier semaphores. Data moves between devices by JAX's collectives and lax.ppermute only.
A program may use at most 128 MiB of HBM per device.

```python
import jax
import jax.numpy as jnp
from jax import lax

BRANCH = 1024
CHAN = 512
TAPS = 4
SPECTRA = 512
FRAMES = 515
INPUTS = 128


def place_ends(array, stream_key, least, top_value):
    extent = array.shape
    place = [jax.random.randint(jax.random.fold_in(stream_key, axis), (), 0, extent[axis]) for axis in range(len(extent))]
    array = array.at[tuple(place)].set(least)
    longest = extent.index(max(extent))
    place[longest] = (place[longest] + 1) % extent[longest]
    return array.at[tuple(place)].set(top_value)


def setup_inputs(seed: int = 0) -> dict:
    seeds = jax.random.split(jax.random.key(seed), 3)
    return {
        "samples": place_ends(jax.random.randint(seeds[0], (INPUTS, FRAMES, BRANCH), -128, 128), jax.random.fold_in(seeds[0], 1), -128, 127).astype(jnp.int32),
        "taps": place_ends(jax.random.randint(seeds[1], (TAPS, BRANCH), -1024, 1025), jax.random.fold_in(seeds[1], 1), -1024, 1024).astype(jnp.int32),
    }


gain_shift = 2.0 ** -21


def filter_bank(samples, taps):
    voltages = samples.astype(jnp.float32)
    weights = taps.astype(jnp.float32)
    filtered = weights[0][None, None, :] * voltages[:, 0:SPECTRA, :]
    for tap_index in range(1, TAPS):
        filtered = filtered + weights[tap_index][None, None, :] * voltages[:, tap_index:tap_index + SPECTRA, :]
    return filtered * gain_shift


def correlate(block):
    real_part = block[0]
    imag_part = block[1]
    gram_real = jnp.dot(real_part, real_part.T, preferred_element_type=jnp.float32) + jnp.dot(imag_part, imag_part.T, preferred_element_type=jnp.float32)
    gram_imag = jnp.dot(imag_part, real_part.T, preferred_element_type=jnp.float32) - jnp.dot(real_part, imag_part.T, preferred_element_type=jnp.float32)
    return jnp.stack([gram_real, gram_imag]) * (1.0 / SPECTRA)


def reference(samples, taps):
    filtered = filter_bank(samples, taps)
    spectrum = jnp.fft.rfft(filtered, axis=-1)[:, :, :CHAN]
    stacked = jnp.stack([jnp.real(spectrum).astype(jnp.bfloat16), jnp.imag(spectrum).astype(jnp.bfloat16)])
    by_channel = jnp.transpose(stacked, (3, 0, 1, 2))
    grams = lax.map(correlate, by_channel)
    return jnp.transpose(grams, (1, 0, 2, 3))
```

```python
import functools
import math

import jax
import jax.numpy as jnp
import numpy as np
from jax import lax
from jax.experimental import pallas as pl
from jax.experimental.pallas import tpu as pltpu
from jax.sharding import PartitionSpec as P

BRANCH = 1024
CHAN = 512
TAPS = 4
SPECTRA = 512
GAIN = 2.0**-21
ROWS = 8
BLOCK = 128


def radix_of(ch_dev):
    return 4 if 2 * ch_dev == 4 * ROWS else 1


def tables(devices, ch_dev):
    radix = radix_of(ch_dev)
    depth = BRANCH // radix
    n = np.arange(depth)
    per = ch_dev // radix
    mats = []
    for residue in range(radix):
        chan = radix * np.arange(CHAN // radix).reshape(devices, per) + residue
        angle = 2.0 * math.pi / BRANCH * ((chan[:, :, None] * n) % BRANCH)
        c, s = np.cos(angle), np.sin(angle)
        if residue == 1:
            re, im = np.concatenate([c, -s], -1), np.concatenate([-s, -c], -1)
        elif residue == 3:
            re, im = np.concatenate([c, s], -1), np.concatenate([-s, c], -1)
        else:
            re, im = c, -s
        mats.append(np.stack([re, im], 1).reshape(devices * 2 * per, -1) * GAIN)
    return mats


def split(x):
    hi = x.astype(jnp.bfloat16)
    return hi, (x - hi.astype(jnp.float32)).astype(jnp.bfloat16)


def split_np(m):
    hi = m.astype(np.float32).astype(jnp.bfloat16)
    return hi, (m - hi.astype(np.float64)).astype(np.float32).astype(jnp.bfloat16)


def product(w, f):
    return lax.dot_general(w, f, (((1,), (1,)), ((), ())), preferred_element_type=jnp.float32)


def filter_kernel(radix, x_ref, taps_ref, *refs):
    w_refs, o_ref, f_ref = refs[:-2], refs[-2], refs[-1]
    rows = o_ref.shape[1]
    taps = taps_ref[...].astype(jnp.float32)
    x = x_ref[...].astype(jnp.float32)
    f = taps[0] * x[0:BLOCK]
    for t in range(1, TAPS):
        f = f + taps[t] * x[t : t + BLOCK]
    f_ref[...] = f
    dests = o_ref.shape[0]
    q = BRANCH // radix
    for i in range(rows):
        fi = f_ref[:, i, :]
        if radix == 4:
            f0, f1, f2, f3 = (fi[:, a * q : (a + 1) * q] for a in range(4))
            even, odd = f0 + f2, f1 + f3
            delta = split(jnp.concatenate([f0 - f2, f1 - f3], 1))
            ops = [split(even + odd), delta, split(even - odd), delta]
        else:
            ops = [split(fi)]
        outs = []
        for r, (hi, lo) in enumerate(ops):
            w_hi, w_lo = w_refs[2 * r][...], w_refs[2 * r + 1][...]
            y = product(w_hi, hi) + (product(w_hi, lo) + product(w_lo, hi))
            outs.append(y.reshape(dests, ROWS, BLOCK))
        o_ref[:, i] = jnp.concatenate(outs, 1).astype(jnp.bfloat16)


def channelise(frames, taps, first, spectra, devices, ch_dev):
    rows = frames.shape[1]
    radix = radix_of(ch_dev)
    mats = [m for w in tables(devices, ch_dev) for m in split_np(w)]
    start = first
    return pl.pallas_call(
        functools.partial(filter_kernel, radix),
        out_shape=jax.ShapeDtypeStruct((devices, rows, 2 * ch_dev, spectra), jnp.bfloat16),
        grid=(spectra // BLOCK,),
        in_specs=[
            pl.BlockSpec(
                (pl.Element(BLOCK + TAPS - 1), pl.Element(rows), pl.Element(BRANCH)),
                lambda j: (start + j * BLOCK, 0, 0),
            ),
            pl.BlockSpec((TAPS, BRANCH), lambda j: (0, 0)),
        ]
        + [pl.BlockSpec(m.shape, lambda j: (0, 0)) for m in mats],
        out_specs=pl.BlockSpec((devices, rows, 2 * ch_dev, BLOCK), lambda j: (0, 0, 0, j)),
        scratch_shapes=[pltpu.VMEM((BLOCK, rows, BRANCH), jnp.float32)],
        compiler_params=pltpu.CompilerParams(vmem_limit_bytes=48 << 20),
        cost_estimate=pl.CostEstimate(flops=6 * spectra * rows * 393216, bytes_accessed=8 << 20, transcendentals=0),
    )(frames, taps, *[jnp.asarray(m) for m in mats])


def gram_kernel(ch_dev, radix, d_ref, p_ref, o_ref, z_ref):
    sources, rows = d_ref.shape[0], d_ref.shape[1]
    span = d_ref.shape[3]
    parts = 2 * ch_dev
    order = p_ref[...]
    for pair in range(sources // 2):
        block = d_ref[2 * pair : 2 * pair + 2].reshape(2 * rows * parts, span)
        turned = jnp.dot(order, block, preferred_element_type=jnp.float32)
        z_ref[:, 2 * rows * pair : 2 * rows * (pair + 1), :] = turned.reshape(parts, 2 * rows, span)
    inputs = sources * rows
    per = ch_dev // radix
    first = pl.program_id(0) == 0
    for c in range(ch_dev):
        at = (c % radix) * 2 * per + c // radix
        z = jnp.concatenate([z_ref[at], z_ref[at + per]], 0).astype(jnp.bfloat16)
        g = product(z, z)
        real = (g[:inputs, :inputs] + g[inputs:, inputs:]) * (1.0 / SPECTRA)
        imag = (g[inputs:, :inputs] - g[:inputs, inputs:]) * (1.0 / SPECTRA)

        @pl.when(first)
        def _():
            o_ref[0, c] = real
            o_ref[1, c] = imag

        @pl.when(jnp.logical_not(first))
        def _():
            o_ref[0, c] += real
            o_ref[1, c] += imag


def correlate(block, ch_dev):
    sources, rows, parts, spectra = block.shape
    radix = radix_of(ch_dev)
    inputs = sources * rows
    span = 256
    wide = 2 * rows * parts
    order = np.zeros((wide, wide), np.float32)
    for a in range(2 * rows):
        for b in range(parts):
            order[b * 2 * rows + a, a * parts + b] = 1.0
    return pl.pallas_call(
        functools.partial(gram_kernel, ch_dev, radix),
        out_shape=jax.ShapeDtypeStruct((2, ch_dev, inputs, inputs), jnp.float32),
        grid=(spectra // span,),
        in_specs=[
            pl.BlockSpec((sources, rows, parts, span), lambda j: (0, 0, 0, j)),
            pl.BlockSpec((wide, wide), lambda j: (0, 0)),
        ],
        out_specs=pl.BlockSpec((2, ch_dev, inputs, inputs), lambda j: (0, 0, 0, 0)),
        scratch_shapes=[pltpu.VMEM((parts, inputs, span), jnp.float32)],
        compiler_params=pltpu.CompilerParams(vmem_limit_bytes=48 << 20),
    )(block, jnp.asarray(order, jnp.bfloat16))


def local(samples, taps):
    groups = lax.axis_size("grp")
    members = lax.axis_size("dev")
    devices = groups * members
    ch_dev = CHAN // devices
    frames = jnp.transpose(samples, (1, 0, 2))
    parcel = channelise(frames, taps, 0, SPECTRA, devices, ch_dev)
    got = lax.all_to_all(parcel, ("grp", "dev"), split_axis=0, concat_axis=0, tiled=True)
    return correlate(got, ch_dev)


def solution(mesh):
    in_specs = (P(("grp", "dev"), None, None), P())
    out_specs = P(None, ("grp", "dev"), None, None)
    return jax.shard_map(local, mesh=mesh, in_specs=in_specs, out_specs=out_specs, check_vma=False)
```

```python
import functools
import math

import jax
import jax.numpy as jnp
import numpy as np
from jax import lax
from jax.experimental import pallas as pl
from jax.experimental.pallas import tpu as pltpu
from jax.sharding import Mesh
from jax.sharding import PartitionSpec as P

BRANCH = 1024
CHAN = 512
TAPS = 4
SPECTRA = 512
GAIN = 2.0**-21
LANES = 128
TILES = BRANCH // LANES
ROWS = 8
BLOCK = 128
AHEAD = 2
STEP = 8
VMEM = 48 << 20

TERMS = {4: (((0, 0),), ((2, 1), (3, 2)), ((1, 3),), ((4, 1), (5, 2))), 1: (((0, 0),),)}


def radix_of(ch_dev):
    return 4 if 2 * ch_dev == 4 * ROWS else 1


def tables(groups, far, near, ch_dev):
    radix = radix_of(ch_dev)
    per = ch_dev // radix
    n = np.arange(BRANCH // radix)
    pieces = []
    for residue in (0, 2, 1, 3) if radix == 4 else (0,):
        chan = radix * np.arange(CHAN // radix).reshape(groups, far, near, per) + residue
        chan = chan.transpose(1, 0, 2, 3)[..., None]
        angle = 2.0 * math.pi / BRANCH * ((chan * n) % BRANCH)
        c, s = np.cos(angle), np.sin(angle)
        if residue == 1:
            pairs = [(c, -s), (-s, -c)]
        elif residue == 3:
            pairs = [(c, -s), (s, c)]
        else:
            pairs = [(c, -s)]
        for re, im in pairs:
            pieces.append(np.stack([re, im], 3).reshape(far, groups * near * 2 * per, -1))
    full = np.stack(pieces) * GAIN
    hi = full.astype(np.float32).astype(jnp.bfloat16)
    lo = (full - hi.astype(np.float64)).astype(np.float32).astype(jnp.bfloat16)
    return np.stack([hi, lo])


def split(x):
    hi = x.astype(jnp.bfloat16)
    return hi, (x - hi.astype(jnp.float32)).astype(jnp.bfloat16)


def product(w, f):
    return lax.dot_general(w, f, (((1,), (1,)), ((), ())), preferred_element_type=jnp.float32)


def filter_kernel(radix, rows, far, me_ref, x_ref, taps_ref, w_ref, *refs):
    outs, f_ref = refs[:-1], refs[-1]
    wide = TILES * rows

    def body(n, carry):
        at = pl.multiple_of(n * STEP, STEP)
        for h in range(0, wide, 8):
            x = x_ref[pl.ds(at, STEP + TAPS - 1), h : h + 8, :].astype(jnp.float32)
            w = taps_ref[:, h : h + 8, :]
            f = w[0] * x[0:STEP]
            for t in range(1, TAPS):
                f = f + w[t] * x[t : t + STEP]
            f_ref[pl.ds(at, STEP), h : h + 8, :] = f
        return carry

    lax.fori_loop(0, BLOCK // STEP, body, 0)
    stride = f_ref.shape[1]
    flat = f_ref.reshape(BLOCK * stride, LANES)
    tiles = TILES // radix
    me = me_ref[0]

    def weights(half, piece):
        return jnp.concatenate([w_ref[half, piece, jnp.bitwise_xor(me, k)] for k in range(far)], 0)

    for first in range(0, rows, 2):
        pair = (first, first + 1)

        def voltage(a):
            return jnp.concatenate(
                [
                    jnp.concatenate(
                        [flat[pl.ds((tiles * a + h) * rows + i, BLOCK, stride=stride), :] for h in range(tiles)], 1
                    )
                    for i in pair
                ],
                0,
            )

        if radix == 4:
            f0, f1, f2, f3 = (voltage(a) for a in range(4))
            even, odd = f0 + f2, f1 + f3
            ops = [split(even + odd), split(f0 - f2), split(f1 - f3), split(even - odd)]
        else:
            ops = [split(voltage(0))]
        sums = []
        for terms in TERMS[radix]:
            y = 0.0
            for piece, at in terms:
                hi, lo = ops[at]
                w_hi, w_lo = weights(0, piece), weights(1, piece)
                y = y + (product(w_hi, hi) + (product(w_hi, lo) + product(w_lo, hi)))
            sums.append(y)
        span = sums[0].shape[0] // far
        for k in range(far):
            for n, i in enumerate(pair):
                part = [
                    y[k * span : (k + 1) * span, n * BLOCK : (n + 1) * BLOCK].reshape(span // ROWS, ROWS, BLOCK)
                    for y in sums
                ]
                block = jnp.concatenate(part, 1).astype(jnp.bfloat16)
                if len(outs) > 1:
                    outs[k][:, i] = block
                else:
                    outs[0][:, 0, k, i] = block


def channelise(me, frames, taps, table, first, blocks, rows, near, ch_dev, apart):
    radix = radix_of(ch_dev)
    far = table.shape[2]
    parts = 2 * ch_dev
    wide = TILES * rows
    if apart:
        out_shape = [jax.ShapeDtypeStruct((near, rows, parts, BLOCK), jnp.bfloat16)] * far
        out_specs = [pl.BlockSpec((near, rows, parts, BLOCK), lambda j, me: (0, 0, 0, 0))] * far
    else:
        out_shape = jax.ShapeDtypeStruct((near, blocks, far, rows, parts, BLOCK), jnp.bfloat16)
        out_specs = pl.BlockSpec((near, 1, far, rows, parts, BLOCK), lambda j, me: (0, j, 0, 0, 0, 0))
    return pl.pallas_call(
        functools.partial(filter_kernel, radix, rows, far),
        out_shape=out_shape,
        grid_spec=pltpu.PrefetchScalarGridSpec(
            num_scalar_prefetch=1,
            grid=(blocks,),
            in_specs=[
                pl.BlockSpec(
                    (pl.Element(BLOCK + TAPS - 1), pl.Element(wide), pl.Element(LANES)),
                    lambda j, me: ((first + j) * BLOCK, 0, 0),
                ),
                pl.BlockSpec(taps.shape, lambda j, me: (0, 0, 0)),
                pl.BlockSpec(table.shape, lambda j, me: (0, 0, 0, 0, 0)),
            ],
            out_specs=out_specs,
            scratch_shapes=[pltpu.VMEM((BLOCK, wide + 8, LANES), jnp.float32)],
        ),
        compiler_params=pltpu.CompilerParams(vmem_limit_bytes=VMEM),
        cost_estimate=pl.CostEstimate(flops=blocks * 3 << 30, bytes_accessed=blocks * 4 << 20, transcendentals=0),
    )(me, frames, taps, table)


def gram_kernel(radix, ch_dev, rows, far, near_size, picks, more, me_ref, order_ref, *refs):
    z_ref, o_ref = refs[-1], refs[-2]
    arrays = refs[:-2]
    if more:
        before, arrays = arrays[0], arrays[1:]
    order = order_ref[...]
    parts = 2 * ch_dev
    both = near_size * rows
    me = me_ref[0]
    for n, pick in enumerate(picks):
        for k in range(far):
            low = pl.multiple_of(jnp.bitwise_xor(me, k) * both, both)
            view = pick(arrays, k)
            for g in range(view.shape[0] // near_size):
                block = view[g * near_size : (g + 1) * near_size].reshape(both * parts, BLOCK)
                turned = jnp.dot(order, block, preferred_element_type=jnp.float32)
                z_ref[:, pl.ds(g * far * both + low, both), n * BLOCK : (n + 1) * BLOCK] = turned.reshape(
                    parts, both, BLOCK
                )
    inputs = z_ref.shape[1]
    per = ch_dev // radix
    for c in range(ch_dev):
        at = (c % radix) * 2 * per + c // radix
        z = jnp.concatenate([z_ref[at], z_ref[at + per]], 0).astype(jnp.bfloat16)
        g = product(z, z)
        real = (g[:inputs, :inputs] + g[inputs:, inputs:]) * (1.0 / SPECTRA)
        imag = (g[inputs:, :inputs] - g[:inputs, inputs:]) * (1.0 / SPECTRA)
        if more:
            real, imag = before[0, c] + real, before[1, c] + imag
        o_ref[0, c] = real
        o_ref[1, c] = imag


def correlate(me, arrays, picks, before, rows, groups, far, near_size, ch_dev):
    parts = 2 * ch_dev
    both = near_size * rows
    wide = both * parts
    order = np.zeros((wide, wide), np.float32)
    for a in range(both):
        for b in range(parts):
            order[b * both + a, a * parts + b] = 1.0
    inputs = groups * far * both
    shape = (2, ch_dev, inputs, inputs)
    args = ([] if before is None else [before]) + list(arrays)
    vmem = pl.BlockSpec(memory_space=pltpu.VMEM)
    return pl.pallas_call(
        functools.partial(gram_kernel, radix_of(ch_dev), ch_dev, rows, far, near_size, picks, before is not None),
        out_shape=jax.ShapeDtypeStruct(shape, jnp.float32),
        in_specs=[pl.BlockSpec(memory_space=pltpu.SMEM)] + [vmem] * (1 + len(args)),
        out_specs=vmem,
        scratch_shapes=[pltpu.VMEM((parts, inputs, len(picks) * BLOCK), jnp.float32)],
        compiler_params=pltpu.CompilerParams(vmem_limit_bytes=VMEM),
        cost_estimate=pl.CostEstimate(flops=3 << 30, bytes_accessed=4 << 20, transcendentals=0),
    )(me, jnp.asarray(order, jnp.bfloat16), *args)


def local(samples, taps):
    rows = samples.shape[0]
    groups, far, near_size = lax.axis_size("grp"), lax.axis_size("far"), lax.axis_size("near")
    near = groups * near_size
    ch_dev = CHAN // (near * far)
    me = lax.axis_index("far").reshape(1)
    count = samples.shape[1]
    frames = samples.reshape(rows, count, TILES, LANES).transpose(1, 2, 0, 3).reshape(count, TILES * rows, LANES)
    weights = taps.astype(jnp.float32).reshape(TAPS, TILES, 1, LANES)
    weights = jnp.broadcast_to(weights, (TAPS, TILES, rows, LANES)).reshape(TAPS, TILES * rows, LANES)
    table = jnp.asarray(tables(groups, far, near_size, ch_dev))
    make = lambda first, blocks, apart: channelise(
        me, frames, weights, table, first, blocks, rows, near, ch_dev, apart
    )
    hops = [k for k in range(far - 1, 0, -1)]
    main = [k for k in hops if k >= far // 2]
    side = [k for k in hops if k < far // 2]
    pairs = lambda k: [(a, a ^ k) for a in range(far)]
    sent = []

    def send(x, k):
        if k in main:
            if len(sent) >= AHEAD:
                x, sent[-AHEAD] = lax.optimization_barrier((x, sent[-AHEAD]))
            sent.append(lax.ppermute(x, "far", pairs(k)))
            return len(sent) - 1
        return lax.ppermute(x, "far", pairs(k))

    def swap(x):
        return lax.all_to_all(x, ("grp", "near"), split_axis=0, concat_axis=0, tiled=True)

    early = [make(0, 1, True), make(1, 1, True)]
    got = []
    for parcel in early:
        got.append({k: send(parcel[k], k) for k in main + side})
    late = swap(make(2, 2, False))
    tail = []
    for n in range(2):
        tail.append({k: send(late[:, n, k], k) for k in main + side})
    arrived = lambda of, k: sent[of[k]] if k in main else of[k]
    first = jnp.stack(
        [
            jnp.stack([early[n][0] if k == 0 else arrived(got[n], k) for k in range(far)], 1)
            for n in range(2)
        ],
        1,
    )
    first = swap(first)
    head = correlate(
        me,
        [first],
        [lambda a, k, n=n: a[0].at[:, n, k] for n in range(2)],
        None,
        rows,
        groups,
        far,
        near_size,
        ch_dev,
    )
    last = [late[:, n, 0] if k == 0 else arrived(tail[n], k) for n in range(2) for k in range(far)]
    return correlate(
        me,
        last,
        [lambda a, k, n=n: a[n * far + k] for n in range(2)],
        head,
        rows,
        groups,
        far,
        near_size,
        ch_dev,
    )


def solution(mesh):
    groups, members = mesh.shape["grp"], mesh.shape["dev"]
    finer = Mesh(mesh.devices.reshape(groups, members // 2, 2), ("grp", "far", "near"))
    whole = ("grp", "far", "near")
    return jax.shard_map(
        local,
        mesh=finer,
        in_specs=(P(whole, None, None), P()),
        out_specs=P(None, whole, None, None),
        check_vma=False,
    )
```

```python
import functools
import math

import jax
import jax.numpy as jnp
import numpy as np
from jax import lax
from jax.experimental import pallas as pl
from jax.experimental.pallas import tpu as pltpu
from jax.sharding import Mesh
from jax.sharding import PartitionSpec as P

BRANCH = 1024
CHAN = 512
TAPS = 4
SPECTRA = 512
GAIN = 2.0**-21
LANES = 128
TILES = BRANCH // LANES
ROWS = 8
BLOCK = 128
EARLY = 1
HEAD_FLOPS = 5 * 10**10
STEP = 8
VMEM = 32 << 20
FILTER_VMEM = 56 << 20

TERMS = {4: (((0, 0),), ((2, 1), (3, 2)), ((1, 3),), ((4, 1), (5, 2))), 1: (((0, 0),),)}


def radix_of(ch_dev):
    return 4 if 2 * ch_dev == 4 * ROWS else 1


def tables(groups, far, near, ch_dev):
    radix = radix_of(ch_dev)
    per = ch_dev // radix
    n = np.arange(BRANCH // radix)
    pieces = []
    for residue in (0, 2, 1, 3) if radix == 4 else (0,):
        chan = radix * np.arange(CHAN // radix).reshape(groups, far, near, per) + residue
        chan = chan.transpose(1, 0, 2, 3)[..., None]
        angle = 2.0 * math.pi / BRANCH * ((chan * n) % BRANCH)
        c, s = np.cos(angle), np.sin(angle)
        if residue == 1:
            pairs = [(c, -s), (-s, -c)]
        elif residue == 3:
            pairs = [(c, -s), (s, c)]
        else:
            pairs = [(c, -s)]
        for re, im in pairs:
            pieces.append(np.stack([re, im], 3).reshape(far, groups * near * 2 * per, -1))
    full = np.stack(pieces) * GAIN
    hi = full.astype(np.float32).astype(jnp.bfloat16)
    lo = (full - hi.astype(np.float64)).astype(np.float32).astype(jnp.bfloat16)
    return np.stack([hi, lo])


def split(x):
    hi = x.astype(jnp.bfloat16)
    return hi, (x - hi.astype(jnp.float32)).astype(jnp.bfloat16)


def product(w, f):
    return lax.dot_general(w, f, (((1,), (1,)), ((), ())), preferred_element_type=jnp.float32)


def filter_kernel(radix, rows, far, apart, me_ref, x_ref, taps_ref, table_ref, *refs):
    outs, (f_ref, turn_ref, taps_f_ref, w_ref, sem) = refs[:-5], refs[-5:]
    wide = TILES * rows
    fetch = pltpu.make_async_copy(table_ref, w_ref, sem)

    @pl.when(pl.program_id(0) == 0)
    def _():
        fetch.start()
        for t in range(TAPS):
            for h in range(TILES):
                tap = taps_ref[t : t + 1, h * LANES : (h + 1) * LANES].astype(jnp.float32)
                taps_f_ref[t, h * rows : (h + 1) * rows, :] = jnp.broadcast_to(tap, (rows, LANES))

    def body(n, carry):
        at = pl.multiple_of(n * STEP, STEP)
        for h in range(0, wide, 8):
            x = x_ref[pl.ds(at, STEP + TAPS - 1), h : h + 8, :].astype(jnp.float32)
            w = taps_f_ref[:, h : h + 8, :]
            f = w[0] * x[0:STEP]
            for t in range(1, TAPS):
                f = f + w[t] * x[t : t + STEP]
            f_ref[pl.ds(at, STEP), h : h + 8, :] = f
        return carry

    lax.fori_loop(0, BLOCK // STEP, body, 0)

    @pl.when(pl.program_id(0) == 0)
    def _():
        fetch.wait()

    stride = f_ref.shape[1]
    flat = f_ref.reshape(BLOCK * stride, LANES)
    tiles = TILES // radix

    def weights(half, piece):
        return jnp.concatenate([w_ref[half, piece, jnp.bitwise_xor(me_ref[0], k)] for k in range(far)], 0)

    for first in range(0, rows, 2):
        pair = (first, first + 1)

        def voltage(a):
            return jnp.concatenate(
                [
                    jnp.concatenate(
                        [flat[pl.ds((tiles * a + h) * rows + i, BLOCK, stride=stride), :] for h in range(tiles)], 1
                    )
                    for i in pair
                ],
                0,
            )

        if radix == 4:
            f0, f1, f2, f3 = (voltage(a) for a in range(4))
            even, odd = f0 + f2, f1 + f3
            ops = [split(even + odd), split(f0 - f2), split(f1 - f3), split(even - odd)]
        else:
            ops = [split(voltage(0))]
        sums = []
        for terms in TERMS[radix]:
            y = 0.0
            for piece, at in terms:
                hi, lo = ops[at]
                w_hi, w_lo = weights(0, piece), weights(1, piece)
                y = y + (product(w_hi, hi) + (product(w_hi, lo) + product(w_lo, hi)))
            sums.append(y)
        span = sums[0].shape[0] // far
        for k in range(far):
            for n, i in enumerate(pair):
                part = [
                    y[k * span : (k + 1) * span, n * BLOCK : (n + 1) * BLOCK].reshape(span // ROWS, ROWS, BLOCK)
                    for y in sums
                ]
                block = jnp.concatenate(part, 1).astype(jnp.bfloat16)
                if apart:
                    turn_ref[k, i] = block
                    for r in range(block.shape[0]):
                        outs[k][r, i] = turn_ref[k, i, jnp.bitwise_xor(me_ref[1], r)]
                else:
                    groups, _, near_size = outs[0].shape[:3]
                    outs[0][:, k, :, 0, i] = block.reshape(groups, near_size, *block.shape[1:])


def channelise(me, frames, taps, table, first, blocks, rows, groups, near_size, ch_dev, apart):
    radix = radix_of(ch_dev)
    far = table.shape[2]
    near = groups * near_size
    parts = 2 * ch_dev
    wide = TILES * rows
    if apart:
        shape = (near, rows, parts, BLOCK)
        out_shape = [jax.ShapeDtypeStruct(shape, jnp.bfloat16)] * far
        out_specs = [pl.BlockSpec(shape, lambda j, me: (0, 0, 0, 0))] * far
    else:
        shape = (groups, far, near_size, blocks, rows, parts, BLOCK)
        out_shape = [jax.ShapeDtypeStruct(shape, jnp.bfloat16)]
        out_specs = [pl.BlockSpec(shape[:3] + (1,) + shape[4:], lambda j, me: (0, 0, 0, j, 0, 0, 0))]
    return pl.pallas_call(
        functools.partial(filter_kernel, radix, rows, far, apart),
        out_shape=out_shape,
        grid_spec=pltpu.PrefetchScalarGridSpec(
            num_scalar_prefetch=1,
            grid=(blocks,),
            in_specs=[
                pl.BlockSpec(
                    (pl.Element(BLOCK + TAPS - 1), pl.Element(wide), pl.Element(LANES)),
                    lambda j, me: ((first + j) * BLOCK, 0, 0),
                ),
                pl.BlockSpec(taps.shape, lambda j, me: (0, 0)),
                pl.BlockSpec(memory_space=pltpu.HBM),
            ],
            out_specs=out_specs,
            scratch_shapes=[
                pltpu.VMEM((BLOCK, wide + 8, LANES), jnp.float32),
                pltpu.VMEM((far, rows, near, parts, BLOCK), jnp.bfloat16),
                pltpu.VMEM((TAPS, wide, LANES), jnp.float32),
                pltpu.VMEM(table.shape, table.dtype),
                pltpu.SemaphoreType.DMA,
            ],
        ),
        compiler_params=pltpu.CompilerParams(vmem_limit_bytes=FILTER_VMEM),
        cost_estimate=pl.CostEstimate(flops=1, bytes_accessed=1, transcendentals=0),
    )(me, frames, taps, table)


def gram_kernel(radix, ch_dev, rows, groups, far, near_size, pick, blocks, more, me_ref, order_ref, *refs):
    z_ref, o_ref = refs[-1], refs[-2]
    arrays = refs[:-2]
    if more:
        before, arrays = arrays[0], arrays[1:]
    parts = 2 * ch_dev
    both = near_size * rows
    me_far, me_near = me_ref[0], me_ref[1]
    me_group = me_near // near_size
    order = order_ref[me_near % near_size]
    for n in range(blocks):
        for k in range(far):
            for g in range(groups):
                at = jnp.bitwise_xor(me_group, g) * far + jnp.bitwise_xor(me_far, k)
                block = jnp.concatenate(
                    [
                        pick(arrays, n, k, g * near_size + x)[...].reshape(rows * parts, BLOCK)
                        for x in range(near_size)
                    ],
                    0,
                )
                turned = jnp.dot(order, block, preferred_element_type=jnp.float32)
                z_ref[:, pl.ds(pl.multiple_of(at * both, both), both), n * BLOCK : (n + 1) * BLOCK] = turned.reshape(
                    parts, both, BLOCK
                )
    inputs = z_ref.shape[1]
    per = ch_dev // radix
    for c in range(ch_dev):
        at = (c % radix) * 2 * per + c // radix
        z = jnp.concatenate([z_ref[at], z_ref[at + per]], 0).astype(jnp.bfloat16)
        g = product(z, z)
        real = (g[:inputs, :inputs] + g[inputs:, inputs:]) * (1.0 / SPECTRA)
        imag = (g[inputs:, :inputs] - g[:inputs, inputs:]) * (1.0 / SPECTRA)
        if more:
            real, imag = before[0, c] + real, before[1, c] + imag
        o_ref[0, c] = real
        o_ref[1, c] = imag


def correlate(me, arrays, pick, blocks, before, flops, rows, groups, far, near_size, ch_dev):
    parts = 2 * ch_dev
    both = near_size * rows
    wide = both * parts
    order = np.zeros((near_size, wide, wide), np.float32)
    for flip in range(near_size):
        for x in range(near_size):
            for i in range(rows):
                for b in range(parts):
                    order[flip, b * both + x * rows + i, ((x ^ flip) * rows + i) * parts + b] = 1.0
    inputs = groups * far * both
    shape = (2, ch_dev, inputs, inputs)
    args = ([] if before is None else [before]) + list(arrays)
    vmem = pl.BlockSpec(memory_space=pltpu.VMEM)
    return pl.pallas_call(
        functools.partial(
            gram_kernel,
            radix_of(ch_dev),
            ch_dev,
            rows,
            groups,
            far,
            near_size,
            pick,
            blocks,
            before is not None,
        ),
        out_shape=jax.ShapeDtypeStruct(shape, jnp.float32),
        in_specs=[pl.BlockSpec(memory_space=pltpu.SMEM)] + [vmem] * (1 + len(args)),
        out_specs=vmem,
        scratch_shapes=[pltpu.VMEM((parts, inputs, blocks * BLOCK), jnp.float32)],
        compiler_params=pltpu.CompilerParams(vmem_limit_bytes=VMEM),
        cost_estimate=pl.CostEstimate(flops=flops, bytes_accessed=1, transcendentals=0),
    )(me, jnp.asarray(order, jnp.bfloat16), *args)


def local(samples, taps):
    rows, count = samples.shape[:2]
    groups, far, near_size = lax.axis_size("grp"), lax.axis_size("far"), lax.axis_size("near")
    near = groups * near_size
    ch_dev = CHAN // (near * far)
    me = jnp.stack([lax.axis_index("far"), lax.axis_index(("grp", "near"))]).astype(jnp.int32)
    origin = jnp.zeros((2,), jnp.int32)
    frames = samples.reshape(rows, count, TILES, LANES).transpose(1, 2, 0, 3).reshape(count, TILES * rows, LANES)
    table = jnp.asarray(tables(groups, far, near_size, ch_dev))
    sizes = (rows, groups, far, near_size, ch_dev)
    rest = SPECTRA // BLOCK - EARLY

    def cross(x, k):
        return lax.ppermute(x, "far", [(a, a ^ k) for a in range(far)])

    def swap(x, r):
        return lax.ppermute(x, ("grp", "near"), [(a, a ^ r) for a in range(near)])

    early = list(channelise(me, frames, taps, table, 0, 1, rows, groups, near_size, ch_dev, True))
    frames, early[0] = lax.optimization_barrier((frames, early[0]))
    (late,) = channelise(origin, frames, taps, table, EARLY, rest, rows, groups, near_size, ch_dev, False)
    late = late.reshape(groups * far * near_size, *late.shape[3:])
    late = lax.all_to_all(late, ("grp", "far", "near"), split_axis=0, concat_axis=0, tiled=True)
    crossed = {k: cross(early[k], k) for k in range(far - 1, 0, -1)}
    crossed[0] = early[0]
    parcel = [jnp.stack([crossed[k][r] for k in range(far)], 0) for r in range(near)]
    first = parcel[:1] + [swap(parcel[r], r) for r in range(1, near)]
    head = correlate(me, first, lambda a, n, k, r: a[r].at[k], 1, None, HEAD_FLOPS, *sizes)
    where = lambda k, r: ((r // near_size) * far + k) * near_size + r % near_size
    return correlate(origin, [late], lambda a, n, k, r: a[0].at[where(k, r), n], rest, head, 1, *sizes)


def solution(mesh):
    groups, members = mesh.shape["grp"], mesh.shape["dev"]
    finer = Mesh(mesh.devices.reshape(groups, members // 2, 2), ("grp", "far", "near"))
    whole = ("grp", "far", "near")
    return jax.shard_map(
        local,
        mesh=finer,
        in_specs=(P(whole, None, None), P()),
        out_specs=P(None, whole, None, None),
        check_vma=False,
    )
```

```python
import functools
import math

import jax
import jax.numpy as jnp
import numpy as np
from jax import lax
from jax.experimental import pallas as pl
from jax.experimental.pallas import tpu as pltpu
from jax.sharding import Mesh
from jax.sharding import PartitionSpec as P

BRANCH = 1024
CHAN = 512
TAPS = 4
SPECTRA = 512
GAIN = 2.0**-21
LANES = 128
TILES = BRANCH // LANES
ROWS = 8
BLOCK = 128
EARLY = 1
HEAD_FLOPS = 5 * 10**10
STEP = 8
PIECES = 4
HEAD_VMEM = 32 << 20
TAIL_VMEM = 50 << 20
FILTER_VMEM = 56 << 20

TERMS = {4: (((0, 0),), ((2, 1), (3, 2)), ((1, 3),), ((4, 1), (5, 2))), 1: (((0, 0),),)}


def radix_of(ch_dev):
    return 4 if 2 * ch_dev == 4 * ROWS else 1


def tables(groups, far, near, ch_dev):
    radix = radix_of(ch_dev)
    per = ch_dev // radix
    n = np.arange(BRANCH // radix)
    pieces = []
    for residue in (0, 2, 1, 3) if radix == 4 else (0,):
        chan = radix * np.arange(CHAN // radix).reshape(groups, far, near, per) + residue
        chan = chan.transpose(1, 0, 2, 3)[..., None]
        angle = 2.0 * math.pi / BRANCH * ((chan * n) % BRANCH)
        c, s = np.cos(angle), np.sin(angle)
        if residue == 1:
            pairs = [(c, -s), (-s, -c)]
        elif residue == 3:
            pairs = [(c, -s), (s, c)]
        else:
            pairs = [(c, -s)]
        for re, im in pairs:
            pieces.append(np.stack([re, im], 3).reshape(far, groups * near * 2 * per, -1))
    full = np.stack(pieces) * GAIN
    hi = full.astype(np.float32).astype(jnp.bfloat16)
    lo = (full - hi.astype(np.float64)).astype(np.float32).astype(jnp.bfloat16)
    return np.stack([hi, lo])


def split(x):
    hi = x.astype(jnp.bfloat16)
    return hi, (x - hi.astype(jnp.float32)).astype(jnp.bfloat16)


def product(w, f):
    return lax.dot_general(w, f, (((1,), (1,)), ((), ())), preferred_element_type=jnp.float32)


def filter_kernel(radix, rows, far, first, blocks, apart, x_ref, taps_ref, table_ref, *refs):
    outs, (f_ref, turn_ref, taps_f_ref, w_ref, held_ref, table_sem, x_sem) = refs[:-7], refs[-7:]
    wide = TILES * rows
    step = pl.program_id(0)
    slot = lax.rem(step, 2)
    size = BLOCK // PIECES
    table_copy = pltpu.make_async_copy(table_ref, w_ref, table_sem)

    def fetch(step, slot, piece):
        low, high = (piece * size + TAPS - 1 if piece else 0), (piece + 1) * size + TAPS - 1
        return pltpu.make_async_copy(
            x_ref.at[pl.ds((first + step) * BLOCK + low, high - low)],
            held_ref.at[slot, low:high],
            x_sem.at[slot, piece],
        )

    @pl.when(step == 0)
    def _():
        for piece in range(PIECES):
            fetch(step, slot, piece).start()
        table_copy.start()
        for t in range(TAPS):
            for h in range(TILES):
                tap = taps_ref[t : t + 1, h * LANES : (h + 1) * LANES].astype(jnp.float32)
                taps_f_ref[t, h * rows : (h + 1) * rows, :] = jnp.broadcast_to(tap, (rows, LANES))

    @pl.when(step + 1 < blocks)
    def _():
        for piece in range(PIECES):
            fetch(step + 1, 1 - slot, piece).start()

    def body(n, carry):
        at = pl.multiple_of(n * STEP, STEP)
        for h in range(0, wide, 8):
            x = held_ref[slot, pl.ds(at, STEP + TAPS - 1), h : h + 8, :].astype(jnp.float32)
            w = taps_f_ref[:, h : h + 8, :]
            f = w[0] * x[0:STEP]
            for t in range(1, TAPS):
                f = f + w[t] * x[t : t + STEP]
            f_ref[pl.ds(at, STEP), h : h + 8, :] = f
        return carry

    for piece in range(PIECES):
        fetch(step, slot, piece).wait()
        lax.fori_loop(piece * size // STEP, (piece + 1) * size // STEP, body, 0)

    @pl.when(step == 0)
    def _():
        table_copy.wait()

    me_far, me_near = (lax.axis_index("far"), lax.axis_index(("grp", "near"))) if apart else (0, 0)
    stride = f_ref.shape[1]
    flat = f_ref.reshape(BLOCK * stride, LANES)
    tiles = TILES // radix

    def weights(half, piece):
        return jnp.concatenate([w_ref[half, piece, me_far ^ k] for k in range(far)], 0)

    for first in range(0, rows, 2):
        pair = (first, first + 1)

        def voltage(a):
            return jnp.concatenate(
                [
                    jnp.concatenate(
                        [flat[pl.ds((tiles * a + h) * rows + i, BLOCK, stride=stride), :] for h in range(tiles)], 1
                    )
                    for i in pair
                ],
                0,
            )

        if radix == 4:
            f0, f1, f2, f3 = (voltage(a) for a in range(4))
            even, odd = f0 + f2, f1 + f3
            ops = [split(even + odd), split(f0 - f2), split(f1 - f3), split(even - odd)]
        else:
            ops = [split(voltage(0))]
        sums = []
        for terms in TERMS[radix]:
            y = 0.0
            for piece, at in terms:
                hi, lo = ops[at]
                w_hi, w_lo = weights(0, piece), weights(1, piece)
                y = y + (product(w_hi, hi) + (product(w_hi, lo) + product(w_lo, hi)))
            sums.append(y)
        span = sums[0].shape[0] // far
        for k in range(far):
            for n, i in enumerate(pair):
                part = [
                    y[k * span : (k + 1) * span, n * BLOCK : (n + 1) * BLOCK].reshape(span // ROWS, ROWS, BLOCK)
                    for y in sums
                ]
                block = jnp.concatenate(part, 1).astype(jnp.bfloat16)
                if apart:
                    turn_ref[k, i] = block
                    for r in range(block.shape[0]):
                        outs[k][r, i] = turn_ref[k, i, me_near ^ r]
                else:
                    groups, _, near_size = outs[0].shape[:3]
                    outs[0][:, k, :, 0, i] = block.reshape(groups, near_size, *block.shape[1:])


def channelise(frames, taps, table, first, blocks, rows, groups, near_size, ch_dev, apart):
    radix = radix_of(ch_dev)
    far = table.shape[2]
    near = groups * near_size
    parts = 2 * ch_dev
    wide = TILES * rows
    if apart:
        shape = (near, rows, parts, BLOCK)
        out_shape = [jax.ShapeDtypeStruct(shape, jnp.bfloat16)] * far
        out_specs = [pl.BlockSpec(shape, lambda j: (0, 0, 0, 0))] * far
    else:
        shape = (groups, far, near_size, blocks, rows, parts, BLOCK)
        out_shape = [jax.ShapeDtypeStruct(shape, jnp.bfloat16)]
        out_specs = [pl.BlockSpec(shape[:3] + (1,) + shape[4:], lambda j: (0, 0, 0, j, 0, 0, 0))]
    return pl.pallas_call(
        functools.partial(filter_kernel, radix, rows, far, first, blocks, apart),
        out_shape=out_shape,
        grid=(blocks,),
        in_specs=[
            pl.BlockSpec(memory_space=pltpu.HBM),
            pl.BlockSpec(taps.shape, lambda j: (0, 0)),
            pl.BlockSpec(memory_space=pltpu.HBM),
        ],
        out_specs=out_specs,
        scratch_shapes=[
            pltpu.VMEM((BLOCK, wide + 8, LANES), jnp.float32),
            pltpu.VMEM((far, rows, near, parts, BLOCK), jnp.bfloat16),
            pltpu.VMEM((TAPS, wide, LANES), jnp.float32),
            pltpu.VMEM(table.shape, table.dtype),
            pltpu.VMEM((2, BLOCK + TAPS - 1, wide, LANES), jnp.int32),
            pltpu.SemaphoreType.DMA,
            pltpu.SemaphoreType.DMA((2, PIECES)),
        ],
        compiler_params=pltpu.CompilerParams(vmem_limit_bytes=FILTER_VMEM),
        cost_estimate=pl.CostEstimate(flops=1, bytes_accessed=1, transcendentals=0),
    )(frames, taps, table)


def gram_kernel(radix, ch_dev, rows, groups, far, near_size, pick, blocks, fixed, more, order_ref, *refs):
    arrays, (o_ref, z_ref, out_ref, old_ref, old_sem, out_sem) = refs[:-6], refs[-6:]
    parts = 2 * ch_dev
    both = near_size * rows
    if more:
        before, arrays = arrays[0], arrays[1:]
        fetch = pltpu.make_async_copy(before, old_ref, old_sem)
        fetch.start()
    if fixed:
        me_far, me_group, me_side = 0, 0, 0
    else:
        me_near = lax.axis_index(("grp", "near"))
        me_far, me_group, me_side = lax.axis_index("far"), me_near // near_size, me_near % near_size
    order = order_ref[me_side]
    wide = 2 if fixed and far % 2 == 0 else 1
    for g in range(groups):
        for k in range(0, far, wide):
            at = (me_group ^ g) * far + (me_far ^ k)
            turned = []
            for w in range(wide):
                block = jnp.concatenate(
                    [
                        jnp.concatenate(
                            [
                                pick(arrays, n, k + w, g * near_size + x)[...].reshape(rows * parts, BLOCK)
                                for x in range(near_size)
                            ],
                            0,
                        )
                        for n in range(blocks)
                    ],
                    1,
                )
                y = jnp.dot(order, block, preferred_element_type=jnp.float32)
                turned.append(y.reshape(parts, both, blocks * BLOCK))
            low = at * both if fixed else pl.multiple_of(at * both, both)
            z_ref[:, pl.ds(low, wide * both), :] = jnp.concatenate(turned, 1).astype(z_ref.dtype)
    inputs = z_ref.shape[1]
    per = ch_dev // radix
    if more:
        fetch.wait()
    copies = []
    for c in range(ch_dev):
        at = (c % radix) * 2 * per + c // radix
        z = jnp.concatenate([z_ref[at], z_ref[at + per]], 0).astype(jnp.bfloat16)
        g = product(z, z)
        real = (g[:inputs, :inputs] + g[inputs:, inputs:]) * (1.0 / SPECTRA)
        imag = (g[inputs:, :inputs] - g[:inputs, inputs:]) * (1.0 / SPECTRA)
        if more:
            real, imag = old_ref[0, c] + real, old_ref[1, c] + imag
        out_ref[0, c] = real
        out_ref[1, c] = imag
        if (c + 1) % radix == 0:
            group = pl.ds(c + 1 - radix, radix)
            copies.append(
                pltpu.make_async_copy(out_ref.at[:, group], o_ref.at[:, group], out_sem.at[c // radix])
            )
            copies[-1].start()
    for copy in copies:
        copy.wait()


def correlate(arrays, pick, blocks, before, fixed, flops, rows, groups, far, near_size, ch_dev):
    parts = 2 * ch_dev
    both = near_size * rows
    wide = both * parts
    order = np.zeros((near_size, wide, wide), np.float32)
    for flip in range(near_size):
        for x in range(near_size):
            for i in range(rows):
                for b in range(parts):
                    order[flip, b * both + x * rows + i, ((x ^ flip) * rows + i) * parts + b] = 1.0
    inputs = groups * far * both
    shape = (2, ch_dev, inputs, inputs)
    vmem, hbm = pl.BlockSpec(memory_space=pltpu.VMEM), pl.BlockSpec(memory_space=pltpu.HBM)
    more = before is not None
    radix = radix_of(ch_dev)
    return pl.pallas_call(
        functools.partial(
            gram_kernel, radix, ch_dev, rows, groups, far, near_size, pick, blocks, fixed, more
        ),
        out_shape=jax.ShapeDtypeStruct(shape, jnp.float32),
        in_specs=[vmem] + [hbm] * more + [vmem] * len(arrays),
        out_specs=hbm,
        scratch_shapes=[
            pltpu.VMEM((parts, inputs, blocks * BLOCK), jnp.bfloat16 if fixed else jnp.float32),
            pltpu.VMEM(shape, jnp.float32),
            pltpu.VMEM(shape if more else (8, LANES), jnp.float32),
            pltpu.SemaphoreType.DMA,
            pltpu.SemaphoreType.DMA((ch_dev // radix,)),
        ],
        compiler_params=pltpu.CompilerParams(vmem_limit_bytes=TAIL_VMEM if more else HEAD_VMEM),
        cost_estimate=pl.CostEstimate(flops=flops, bytes_accessed=1, transcendentals=0),
    )(jnp.asarray(order, jnp.bfloat16), *([before] if more else []), *arrays)


def local(samples, taps):
    rows, count = samples.shape[:2]
    groups, far, near_size = lax.axis_size("grp"), lax.axis_size("far"), lax.axis_size("near")
    near = groups * near_size
    ch_dev = CHAN // (near * far)
    frames = samples.reshape(rows, count, TILES, LANES).transpose(1, 2, 0, 3).reshape(count, TILES * rows, LANES)
    table = jnp.asarray(tables(groups, far, near_size, ch_dev))
    sizes = (rows, groups, far, near_size, ch_dev)
    rest = SPECTRA // BLOCK - EARLY

    def cross(x, k):
        return lax.ppermute(x, "far", [(a, a ^ k) for a in range(far)])

    def swap(x, r):
        return lax.ppermute(x, ("grp", "near"), [(a, a ^ r) for a in range(near)])

    early = list(channelise(frames, taps, table, 0, 1, rows, groups, near_size, ch_dev, True))
    frames, early[0] = lax.optimization_barrier((frames, early[0]))
    (late,) = channelise(frames, taps, table, EARLY, rest, rows, groups, near_size, ch_dev, False)
    late = late.reshape(groups * far * near_size, *late.shape[3:])
    late = lax.all_to_all(late, ("grp", "far", "near"), split_axis=0, concat_axis=0, tiled=True)
    crossed = {k: cross(early[k], k) for k in range(far - 1, 0, -1)}
    crossed[0] = early[0]
    parcel = [jnp.stack([crossed[k][r] for k in range(far)], 0) for r in range(near)]
    first = parcel[:1] + [swap(parcel[r], r) for r in range(1, near)]
    head = correlate(first, lambda a, n, k, r: a[r].at[k], 1, None, False, HEAD_FLOPS, *sizes)
    where = lambda k, r: ((r // near_size) * far + k) * near_size + r % near_size
    return correlate([late], lambda a, n, k, r: a[0].at[where(k, r), n], rest, head, True, 1, *sizes)


def solution(mesh):
    groups, members = mesh.shape["grp"], mesh.shape["dev"]
    finer = Mesh(mesh.devices.reshape(groups, members // 2, 2), ("grp", "far", "near"))
    whole = ("grp", "far", "near")
    return jax.shard_map(
        local,
        mesh=finer,
        in_specs=(P(whole, None, None), P()),
        out_specs=P(None, whole, None, None),
        check_vma=False,
    )
```

```python
import functools
import math

import jax
import jax.numpy as jnp
import numpy as np
from jax import lax
from jax.experimental import pallas as pl
from jax.experimental.pallas import tpu as pltpu
from jax.sharding import Mesh
from jax.sharding import PartitionSpec as P

BRANCH = 1024
CHAN = 512
TAPS = 4
SPECTRA = 512
GAIN = 2.0**-21
LANES = 128
TILES = BRANCH // LANES
ROWS = 8
BLOCK = 128
EARLY = 1
HEAD_FLOPS = 5 * 10**10
GROUP = 4
STEP = 8
PIECES = 4
HEAD_VMEM = 32 << 20
TAIL_VMEM = 32 << 20
FILTER_VMEM = 56 << 20

TERMS = {4: (((0, 0),), ((2, 1), (3, 2)), ((1, 3),), ((4, 1), (5, 2))), 1: (((0, 0),),)}


def radix_of(ch_dev):
    return 4 if 2 * ch_dev == 4 * ROWS else 1


def tables(groups, far, near, ch_dev):
    radix = radix_of(ch_dev)
    per = ch_dev // radix
    n = np.arange(BRANCH // radix)
    pieces = []
    for residue in (0, 2, 1, 3) if radix == 4 else (0,):
        chan = radix * np.arange(CHAN // radix).reshape(groups, far, near, per) + residue
        chan = chan.transpose(1, 0, 2, 3)[..., None]
        angle = 2.0 * math.pi / BRANCH * ((chan * n) % BRANCH)
        c, s = np.cos(angle), np.sin(angle)
        if residue == 1:
            pairs = [(c, -s), (-s, -c)]
        elif residue == 3:
            pairs = [(c, -s), (s, c)]
        else:
            pairs = [(c, -s)]
        for re, im in pairs:
            pieces.append(np.stack([re, im], 3).reshape(far, groups * near * 2 * per, -1))
    full = np.stack(pieces) * GAIN
    hi = full.astype(np.float32).astype(jnp.bfloat16)
    lo = (full - hi.astype(np.float64)).astype(np.float32).astype(jnp.bfloat16)
    return np.stack([hi, lo])


def split(x):
    hi = x.astype(jnp.bfloat16)
    return hi, (x - hi.astype(jnp.float32)).astype(jnp.bfloat16)


def product(w, f):
    return lax.dot_general(w, f, (((1,), (1,)), ((), ())), preferred_element_type=jnp.float32)


def filter_kernel(radix, rows, far, first, blocks, apart, x_ref, taps_ref, table_ref, *refs):
    outs, (f_ref, turn_ref, taps_f_ref, w_ref, held_ref, table_sem, x_sem) = refs[:-7], refs[-7:]
    wide = TILES * rows
    step = pl.program_id(0)
    slot = lax.rem(step, 2)
    size = BLOCK // PIECES
    table_copy = pltpu.make_async_copy(table_ref, w_ref, table_sem)

    def fetch(step, slot, piece):
        low, high = (piece * size + TAPS - 1 if piece else 0), (piece + 1) * size + TAPS - 1
        return pltpu.make_async_copy(
            x_ref.at[pl.ds((first + step) * BLOCK + low, high - low)],
            held_ref.at[slot, low:high],
            x_sem.at[slot, piece],
        )

    @pl.when(step == 0)
    def _():
        for piece in range(PIECES):
            fetch(step, slot, piece).start()
        table_copy.start()
        for t in range(TAPS):
            for h in range(TILES):
                tap = taps_ref[t : t + 1, h * LANES : (h + 1) * LANES].astype(jnp.float32)
                taps_f_ref[t, h * rows : (h + 1) * rows, :] = jnp.broadcast_to(tap, (rows, LANES))

    @pl.when(step + 1 < blocks)
    def _():
        for piece in range(PIECES):
            fetch(step + 1, 1 - slot, piece).start()

    def body(n, carry):
        at = pl.multiple_of(n * STEP, STEP)
        for h in range(0, wide, 8):
            x = held_ref[slot, pl.ds(at, STEP + TAPS - 1), h : h + 8, :].astype(jnp.float32)
            w = taps_f_ref[:, h : h + 8, :]
            f = w[0] * x[0:STEP]
            for t in range(1, TAPS):
                f = f + w[t] * x[t : t + STEP]
            f_ref[pl.ds(at, STEP), h : h + 8, :] = f
        return carry

    for piece in range(PIECES):
        fetch(step, slot, piece).wait()
        lax.fori_loop(piece * size // STEP, (piece + 1) * size // STEP, body, 0)

    @pl.when(step == 0)
    def _():
        table_copy.wait()

    me_far, me_near = (lax.axis_index("far"), lax.axis_index(("grp", "near"))) if apart else (0, 0)
    stride = f_ref.shape[1]
    flat = f_ref.reshape(BLOCK * stride, LANES)
    tiles = TILES // radix

    def weights(half, piece):
        return jnp.concatenate([w_ref[half, piece, me_far ^ k] for k in range(far)], 0)

    for first in range(0, rows, 2):
        pair = (first, first + 1)

        def voltage(a):
            return jnp.concatenate(
                [
                    jnp.concatenate(
                        [flat[pl.ds((tiles * a + h) * rows + i, BLOCK, stride=stride), :] for h in range(tiles)], 1
                    )
                    for i in pair
                ],
                0,
            )

        if radix == 4:
            f0, f1, f2, f3 = (voltage(a) for a in range(4))
            even, odd = f0 + f2, f1 + f3
            ops = [split(even + odd), split(f0 - f2), split(f1 - f3), split(even - odd)]
        else:
            ops = [split(voltage(0))]
        sums = []
        for terms in TERMS[radix]:
            y = 0.0
            for piece, at in terms:
                hi, lo = ops[at]
                w_hi, w_lo = weights(0, piece), weights(1, piece)
                y = y + (product(w_hi, hi) + (product(w_hi, lo) + product(w_lo, hi)))
            sums.append(y)
        span = sums[0].shape[0] // far
        for k in range(far):
            for n, i in enumerate(pair):
                part = [
                    y[k * span : (k + 1) * span, n * BLOCK : (n + 1) * BLOCK].reshape(span // ROWS, ROWS, BLOCK)
                    for y in sums
                ]
                block = jnp.concatenate(part, 1).astype(jnp.bfloat16)
                if apart:
                    turn_ref[k, i] = block
                    for r in range(block.shape[0]):
                        outs[k][r, i] = turn_ref[k, i, me_near ^ r]
                else:
                    groups, _, near_size = outs[0].shape[:3]
                    outs[0][:, k, :, 0, i] = block.reshape(groups, near_size, *block.shape[1:])


def channelise(frames, taps, table, first, blocks, rows, groups, near_size, ch_dev, apart):
    radix = radix_of(ch_dev)
    far = table.shape[2]
    near = groups * near_size
    parts = 2 * ch_dev
    wide = TILES * rows
    if apart:
        shape = (near, rows, parts, BLOCK)
        out_shape = [jax.ShapeDtypeStruct(shape, jnp.bfloat16)] * far
        out_specs = [pl.BlockSpec(shape, lambda j: (0, 0, 0, 0))] * far
    else:
        shape = (groups, far, near_size, blocks, rows, parts, BLOCK)
        out_shape = [jax.ShapeDtypeStruct(shape, jnp.bfloat16)]
        out_specs = [pl.BlockSpec(shape[:3] + (1,) + shape[4:], lambda j: (0, 0, 0, j, 0, 0, 0))]
    return pl.pallas_call(
        functools.partial(filter_kernel, radix, rows, far, first, blocks, apart),
        out_shape=out_shape,
        grid=(blocks,),
        in_specs=[
            pl.BlockSpec(memory_space=pltpu.HBM),
            pl.BlockSpec(taps.shape, lambda j: (0, 0)),
            pl.BlockSpec(memory_space=pltpu.HBM),
        ],
        out_specs=out_specs,
        scratch_shapes=[
            pltpu.VMEM((BLOCK, wide + 8, LANES), jnp.float32),
            pltpu.VMEM((far, rows, near, parts, BLOCK), jnp.bfloat16),
            pltpu.VMEM((TAPS, wide, LANES), jnp.float32),
            pltpu.VMEM(table.shape, table.dtype),
            pltpu.VMEM((2, BLOCK + TAPS - 1, wide, LANES), jnp.int32),
            pltpu.SemaphoreType.DMA,
            pltpu.SemaphoreType.DMA((2, PIECES)),
        ],
        compiler_params=pltpu.CompilerParams(vmem_limit_bytes=FILTER_VMEM),
        cost_estimate=pl.CostEstimate(flops=1, bytes_accessed=1, transcendentals=0),
    )(frames, taps, table)


def turn(order, views, rows, parts, both):
    blocks = [jnp.concatenate([v[...].reshape(rows * parts, BLOCK) for v in near], 0) for near in views]
    y = jnp.dot(order, jnp.concatenate(blocks, 1), preferred_element_type=jnp.float32)
    return y.reshape(parts, both, len(views) * BLOCK)


def head_kernel(rows, groups, far, near_size, parts, order_ref, *refs):
    arrays, (o_ref, z_ref) = refs[:-2], refs[-2:]
    both = near_size * rows
    me_near, me_far = lax.axis_index(("grp", "near")), lax.axis_index("far")
    me_group, me_side = me_near // near_size, me_near % near_size
    order = order_ref[me_side]
    for g in range(groups):
        for k in range(far):
            at = (me_group ^ g) * far + (me_far ^ k)
            near = [arrays[g * near_size + x].at[k] for x in range(near_size)]
            z_ref[:, pl.ds(pl.multiple_of(at * both, both), both), :] = turn(order, [near], rows, parts, both)
    o_ref[...] = z_ref[...].astype(o_ref.dtype)


def gram_kernel(radix, ch_dev, rows, groups, far, near_size, order_ref, early_ref, late_ref, *refs):
    o_ref, z_ref, out_ref, early_sem, out_sem = refs
    parts = 2 * ch_dev
    both = near_size * rows
    pieces = early_sem.shape[0]
    size = parts // pieces
    fetches = []
    for n in range(pieces):
        part = pl.ds(n * size, size)
        fetches.append(pltpu.make_async_copy(early_ref.at[part], z_ref.at[part, :, 0:BLOCK], early_sem.at[n]))
        fetches[-1].start()
    order = order_ref[0]
    wide = 2 if far % 2 == 0 else 1
    for g in range(groups):
        for k in range(0, far, wide):
            turned = []
            for w in range(wide):
                at = (g * far + k + w) * near_size
                views = [
                    [late_ref.at[at + x, n] for x in range(near_size)] for n in range(late_ref.shape[1])
                ]
                turned.append(turn(order, views, rows, parts, both))
            low = (g * far + k) * both
            z_ref[:, low : low + wide * both, BLOCK:] = jnp.concatenate(turned, 1).astype(z_ref.dtype)
    for fetch in fetches:
        fetch.wait()
    inputs = z_ref.shape[1]
    per = ch_dev // radix
    copies = []
    for c in range(ch_dev):
        at = (c % radix) * 2 * per + c // radix
        z = jnp.concatenate([z_ref[at], z_ref[at + per]], 0)
        g = product(z, z)
        out_ref[0, c] = (g[:inputs, :inputs] + g[inputs:, inputs:]) * (1.0 / SPECTRA)
        out_ref[1, c] = (g[inputs:, :inputs] - g[:inputs, inputs:]) * (1.0 / SPECTRA)
        if (c + 1) % GROUP == 0:
            group = pl.ds(c + 1 - GROUP, GROUP)
            copies.append(
                pltpu.make_async_copy(out_ref.at[:, group], o_ref.at[:, group], out_sem.at[c // GROUP])
            )
            copies[-1].start()
    for copy in copies:
        copy.wait()


def order_of(rows, near_size, parts):
    both = near_size * rows
    wide = both * parts
    order = np.zeros((near_size, wide, wide), np.float32)
    for flip in range(near_size):
        for x in range(near_size):
            for i in range(rows):
                for b in range(parts):
                    order[flip, b * both + x * rows + i, ((x ^ flip) * rows + i) * parts + b] = 1.0
    return jnp.asarray(order, jnp.bfloat16)


def collect(arrays, rows, groups, far, near_size, ch_dev):
    parts, inputs = 2 * ch_dev, groups * far * near_size * rows
    vmem = pl.BlockSpec(memory_space=pltpu.VMEM)
    return pl.pallas_call(
        functools.partial(head_kernel, rows, groups, far, near_size, parts),
        out_shape=jax.ShapeDtypeStruct((parts, inputs, BLOCK), jnp.bfloat16),
        in_specs=[vmem] * (1 + len(arrays)),
        out_specs=vmem,
        scratch_shapes=[pltpu.VMEM((parts, inputs, BLOCK), jnp.float32)],
        compiler_params=pltpu.CompilerParams(vmem_limit_bytes=HEAD_VMEM),
        cost_estimate=pl.CostEstimate(flops=HEAD_FLOPS, bytes_accessed=1, transcendentals=0),
    )(order_of(rows, near_size, parts), *arrays)


def correlate(early, late, rows, groups, far, near_size, ch_dev):
    parts, inputs = 2 * ch_dev, groups * far * near_size * rows
    shape = (2, ch_dev, inputs, inputs)
    vmem, hbm = pl.BlockSpec(memory_space=pltpu.VMEM), pl.BlockSpec(memory_space=pltpu.HBM)
    return pl.pallas_call(
        functools.partial(gram_kernel, radix_of(ch_dev), ch_dev, rows, groups, far, near_size),
        out_shape=jax.ShapeDtypeStruct(shape, jnp.float32),
        in_specs=[vmem, hbm, vmem],
        out_specs=hbm,
        scratch_shapes=[
            pltpu.VMEM((parts, inputs, SPECTRA), jnp.bfloat16),
            pltpu.VMEM(shape, jnp.float32),
            pltpu.SemaphoreType.DMA((4,)),
            pltpu.SemaphoreType.DMA((ch_dev // GROUP,)),
        ],
        compiler_params=pltpu.CompilerParams(vmem_limit_bytes=TAIL_VMEM),
        cost_estimate=pl.CostEstimate(flops=1, bytes_accessed=1, transcendentals=0),
    )(order_of(rows, near_size, parts), pltpu.with_memory_space_constraint(early, pltpu.HBM), late)


def local(samples, taps):
    rows, count = samples.shape[:2]
    groups, far, near_size = lax.axis_size("grp"), lax.axis_size("far"), lax.axis_size("near")
    near = groups * near_size
    ch_dev = CHAN // (near * far)
    frames = samples.reshape(rows, count, TILES, LANES).transpose(1, 2, 0, 3).reshape(count, TILES * rows, LANES)
    table = jnp.asarray(tables(groups, far, near_size, ch_dev))
    sizes = (rows, groups, far, near_size, ch_dev)
    rest = SPECTRA // BLOCK - EARLY

    def cross(x, k):
        return lax.ppermute(x, "far", [(a, a ^ k) for a in range(far)])

    def swap(x, r):
        return lax.ppermute(x, ("grp", "near"), [(a, a ^ r) for a in range(near)])

    early = list(channelise(frames, taps, table, 0, 1, rows, groups, near_size, ch_dev, True))
    frames, early[0] = lax.optimization_barrier((frames, early[0]))
    (late,) = channelise(frames, taps, table, EARLY, rest, rows, groups, near_size, ch_dev, False)
    late = late.reshape(groups * far * near_size, *late.shape[3:])
    late = lax.all_to_all(late, ("grp", "far", "near"), split_axis=0, concat_axis=0, tiled=True)
    crossed = {k: cross(early[k], k) for k in range(far - 1, 0, -1)}
    crossed[0] = early[0]
    parcel = [jnp.stack([crossed[k][r] for k in range(far)], 0) for r in range(near)]
    first = parcel[:1] + [swap(parcel[r], r) for r in range(1, near)]
    return correlate(collect(first, *sizes), late, *sizes)


def solution(mesh):
    groups, members = mesh.shape["grp"], mesh.shape["dev"]
    finer = Mesh(mesh.devices.reshape(groups, members // 2, 2), ("grp", "far", "near"))
    whole = ("grp", "far", "near")
    return jax.shard_map(
        local,
        mesh=finer,
        in_specs=(P(whole, None, None), P()),
        out_specs=P(None, whole, None, None),
        check_vma=False,
    )
```

```python
import functools
import math

import jax
import jax.numpy as jnp
import numpy as np
from jax import lax
from jax.experimental import pallas as pl
from jax.experimental.pallas import tpu as pltpu
from jax.sharding import Mesh
from jax.sharding import PartitionSpec as P

BRANCH = 1024
CHAN = 512
TAPS = 4
SPECTRA = 512
GAIN = 2.0**-21
LANES = 128
TILES = BRANCH // LANES
ROWS = 8
BLOCK = 128
EARLY = 1
HEAD_FLOPS = 5 * 10**10
GROUP = 4
STEP = 8
PIECES = 2
HEAD_VMEM = 32 << 20
TAIL_VMEM = 32 << 20
FILTER_VMEM = 56 << 20

TERMS = {4: (((0, 0),), ((2, 1), (3, 2)), ((1, 3),), ((4, 1), (5, 2))), 1: (((0, 0),),)}


def radix_of(ch_dev):
    return 4 if 2 * ch_dev == 4 * ROWS else 1


def tables(groups, far, near, ch_dev):
    radix = radix_of(ch_dev)
    per = ch_dev // radix
    n = np.arange(BRANCH // radix)
    pieces = []
    for residue in (0, 2, 1, 3) if radix == 4 else (0,):
        chan = radix * np.arange(CHAN // radix).reshape(groups, far, near, per) + residue
        chan = chan.transpose(1, 0, 2, 3)[..., None]
        angle = 2.0 * math.pi / BRANCH * ((chan * n) % BRANCH)
        c, s = np.cos(angle), np.sin(angle)
        if residue == 1:
            pairs = [(c, -s), (-s, -c)]
        elif residue == 3:
            pairs = [(c, -s), (s, c)]
        else:
            pairs = [(c, -s)]
        for re, im in pairs:
            pieces.append(np.stack([re, im], 3).reshape(far, groups * near * 2 * per, -1))
    full = np.stack(pieces) * GAIN
    hi = full.astype(np.float32).astype(jnp.bfloat16)
    lo = (full - hi.astype(np.float64)).astype(np.float32).astype(jnp.bfloat16)
    return np.stack([hi, lo])


def split(x):
    hi = x.astype(jnp.bfloat16)
    return hi, (x - hi.astype(jnp.float32)).astype(jnp.bfloat16)


def product(w, f):
    return lax.dot_general(w, f, (((1,), (1,)), ((), ())), preferred_element_type=jnp.float32)


def filter_kernel(radix, rows, far, first, blocks, apart, x_ref, taps_ref, table_ref, *refs):
    outs, (f_ref, turn_ref, taps_f_ref, w_ref, held_ref, table_sem, x_sem) = refs[:-7], refs[-7:]
    wide = TILES * rows
    step = pl.program_id(0)
    slot = lax.rem(step, 2)
    size = BLOCK // PIECES
    table_copies = [
        pltpu.make_async_copy(table_ref.at[half, n], w_ref.at[half, n], table_sem.at[half, n])
        for n in range(w_ref.shape[1])
        for half in range(2)
    ]

    def fetch(step, slot, piece):
        low, high = (piece * size + TAPS - 1 if piece else 0), (piece + 1) * size + TAPS - 1
        return pltpu.make_async_copy(
            x_ref.at[pl.ds((first + step) * BLOCK + low, high - low)],
            held_ref.at[slot, low:high],
            x_sem.at[slot, piece],
        )

    @pl.when(step == 0)
    def _():
        for piece in range(PIECES):
            fetch(step, slot, piece).start()
        for copy in table_copies:
            copy.start()
        for t in range(TAPS):
            for h in range(TILES):
                tap = taps_ref[t : t + 1, h * LANES : (h + 1) * LANES].astype(jnp.float32)
                taps_f_ref[t, h * rows : (h + 1) * rows, :] = jnp.broadcast_to(tap, (rows, LANES))

    @pl.when(step + 1 < blocks)
    def _():
        for piece in range(PIECES):
            fetch(step + 1, 1 - slot, piece).start()

    def body(n, carry):
        at = pl.multiple_of(n * STEP, STEP)
        for h in range(0, wide, 8):
            x = held_ref[slot, pl.ds(at, STEP + TAPS - 1), h : h + 8, :].astype(jnp.float32)
            w = taps_f_ref[:, h : h + 8, :]
            f = w[0] * x[0:STEP]
            for t in range(1, TAPS):
                f = f + w[t] * x[t : t + STEP]
            f_ref[pl.ds(at, STEP), h : h + 8, :] = f
        return carry

    for piece in range(PIECES):
        fetch(step, slot, piece).wait()
        lax.fori_loop(piece * size // STEP, (piece + 1) * size // STEP, body, 0)

    @pl.when(step == 0)
    def _():
        for copy in table_copies:
            copy.wait()

    me_far, me_near = (lax.axis_index("far"), lax.axis_index(("grp", "near"))) if apart else (0, 0)
    stride = f_ref.shape[1]
    flat = f_ref.reshape(BLOCK * stride, LANES)
    tiles = TILES // radix

    def weights(half, piece):
        return jnp.concatenate([w_ref[half, piece, me_far ^ k] for k in range(far)], 0)

    for first in range(0, rows, 2):
        pair = (first, first + 1)

        def voltage(a):
            return jnp.concatenate(
                [
                    jnp.concatenate(
                        [flat[pl.ds((tiles * a + h) * rows + i, BLOCK, stride=stride), :] for h in range(tiles)], 1
                    )
                    for i in pair
                ],
                0,
            )

        if radix == 4:
            f0, f1, f2, f3 = (voltage(a) for a in range(4))
            even, odd = f0 + f2, f1 + f3
            ops = [split(even + odd), split(f0 - f2), split(f1 - f3), split(even - odd)]
        else:
            ops = [split(voltage(0))]
        sums = []
        for terms in TERMS[radix]:
            y = 0.0
            for piece, at in terms:
                hi, lo = ops[at]
                w_hi, w_lo = weights(0, piece), weights(1, piece)
                y = y + (product(w_hi, hi) + (product(w_hi, lo) + product(w_lo, hi)))
            sums.append(y)
        span = sums[0].shape[0] // far
        for k in range(far):
            for n, i in enumerate(pair):
                part = [
                    y[k * span : (k + 1) * span, n * BLOCK : (n + 1) * BLOCK].reshape(span // ROWS, ROWS, BLOCK)
                    for y in sums
                ]
                block = jnp.concatenate(part, 1).astype(jnp.bfloat16)
                if apart:
                    turn_ref[k, i] = block
                    for r in range(block.shape[0]):
                        outs[k][r, i] = turn_ref[k, i, me_near ^ r]
                else:
                    groups, _, near_size = outs[0].shape[:3]
                    outs[0][:, k, :, 0, i] = block.reshape(groups, near_size, *block.shape[1:])


def channelise(frames, taps, table, first, blocks, rows, groups, near_size, ch_dev, apart):
    radix = radix_of(ch_dev)
    far = table.shape[2]
    near = groups * near_size
    parts = 2 * ch_dev
    wide = TILES * rows
    if apart:
        shape = (near, rows, parts, BLOCK)
        out_shape = [jax.ShapeDtypeStruct(shape, jnp.bfloat16)] * far
        out_specs = [pl.BlockSpec(shape, lambda j: (0, 0, 0, 0))] * far
    else:
        shape = (groups, far, near_size, blocks, rows, parts, BLOCK)
        out_shape = [jax.ShapeDtypeStruct(shape, jnp.bfloat16)]
        out_specs = [pl.BlockSpec(shape[:3] + (1,) + shape[4:], lambda j: (0, 0, 0, j, 0, 0, 0))]
    return pl.pallas_call(
        functools.partial(filter_kernel, radix, rows, far, first, blocks, apart),
        out_shape=out_shape,
        grid=(blocks,),
        in_specs=[
            pl.BlockSpec(memory_space=pltpu.HBM),
            pl.BlockSpec(taps.shape, lambda j: (0, 0)),
            pl.BlockSpec(memory_space=pltpu.HBM),
        ],
        out_specs=out_specs,
        scratch_shapes=[
            pltpu.VMEM((BLOCK, wide + 8, LANES), jnp.float32),
            pltpu.VMEM((far, rows, near, parts, BLOCK), jnp.bfloat16),
            pltpu.VMEM((TAPS, wide, LANES), jnp.float32),
            pltpu.VMEM(table.shape, table.dtype),
            pltpu.VMEM((2, BLOCK + TAPS - 1, wide, LANES), jnp.int32),
            pltpu.SemaphoreType.DMA(table.shape[:2]),
            pltpu.SemaphoreType.DMA((2, PIECES)),
        ],
        compiler_params=pltpu.CompilerParams(vmem_limit_bytes=FILTER_VMEM),
        cost_estimate=pl.CostEstimate(flops=1, bytes_accessed=1, transcendentals=0),
    )(frames, taps, table)


def turn(order, views, rows, parts, both):
    blocks = [jnp.concatenate([v[...].reshape(rows * parts, BLOCK) for v in near], 0) for near in views]
    y = jnp.dot(order, jnp.concatenate(blocks, 1), preferred_element_type=jnp.float32)
    return y.reshape(parts, both, len(views) * BLOCK)


def head_kernel(rows, groups, far, near_size, parts, order_ref, *refs):
    arrays, (o_ref, z_ref) = refs[:-2], refs[-2:]
    both = near_size * rows
    me_near, me_far = lax.axis_index(("grp", "near")), lax.axis_index("far")
    me_group, me_side = me_near // near_size, me_near % near_size
    order = order_ref[me_side]
    for g in range(groups):
        for k in range(far):
            at = (me_group ^ g) * far + (me_far ^ k)
            near = [arrays[g * near_size + x].at[k] for x in range(near_size)]
            z_ref[:, pl.ds(pl.multiple_of(at * both, both), both), :] = turn(order, [near], rows, parts, both)
    o_ref[...] = z_ref[...].astype(o_ref.dtype)


def gram_kernel(radix, ch_dev, rows, groups, far, near_size, order_ref, early_ref, late_ref, *refs):
    o_ref, z_ref, out_ref, early_sem, out_sem = refs
    parts = 2 * ch_dev
    both = near_size * rows
    pieces = early_sem.shape[0]
    size = parts // pieces
    fetches = []
    for n in range(pieces):
        part = pl.ds(n * size, size)
        fetches.append(pltpu.make_async_copy(early_ref.at[part], z_ref.at[part, :, 0:BLOCK], early_sem.at[n]))
        fetches[-1].start()
    order = order_ref[0]
    wide = 2 if far % 2 == 0 else 1
    for g in range(groups):
        for k in range(0, far, wide):
            turned = []
            for w in range(wide):
                at = (g * far + k + w) * near_size
                views = [
                    [late_ref.at[at + x, n] for x in range(near_size)] for n in range(late_ref.shape[1])
                ]
                turned.append(turn(order, views, rows, parts, both))
            low = (g * far + k) * both
            z_ref[:, low : low + wide * both, BLOCK:] = jnp.concatenate(turned, 1).astype(z_ref.dtype)
    for fetch in fetches:
        fetch.wait()
    inputs = z_ref.shape[1]
    per = ch_dev // radix
    copies = []
    for c in range(ch_dev):
        at = (c % radix) * 2 * per + c // radix
        z = jnp.concatenate([z_ref[at], z_ref[at + per]], 0)
        g = product(z, z)
        out_ref[0, c] = (g[:inputs, :inputs] + g[inputs:, inputs:]) * (1.0 / SPECTRA)
        out_ref[1, c] = (g[inputs:, :inputs] - g[:inputs, inputs:]) * (1.0 / SPECTRA)
        if (c + 1) % GROUP == 0:
            group = pl.ds(c + 1 - GROUP, GROUP)
            copies.append(
                pltpu.make_async_copy(out_ref.at[:, group], o_ref.at[:, group], out_sem.at[c // GROUP])
            )
            copies[-1].start()
    for copy in copies:
        copy.wait()


def order_of(rows, near_size, parts):
    both = near_size * rows
    wide = both * parts
    order = np.zeros((near_size, wide, wide), np.float32)
    for flip in range(near_size):
        for x in range(near_size):
            for i in range(rows):
                for b in range(parts):
                    order[flip, b * both + x * rows + i, ((x ^ flip) * rows + i) * parts + b] = 1.0
    return jnp.asarray(order, jnp.bfloat16)


def collect(arrays, rows, groups, far, near_size, ch_dev):
    parts, inputs = 2 * ch_dev, groups * far * near_size * rows
    vmem = pl.BlockSpec(memory_space=pltpu.VMEM)
    return pl.pallas_call(
        functools.partial(head_kernel, rows, groups, far, near_size, parts),
        out_shape=jax.ShapeDtypeStruct((parts, inputs, BLOCK), jnp.bfloat16),
        in_specs=[vmem] * (1 + len(arrays)),
        out_specs=vmem,
        scratch_shapes=[pltpu.VMEM((parts, inputs, BLOCK), jnp.float32)],
        compiler_params=pltpu.CompilerParams(vmem_limit_bytes=HEAD_VMEM),
        cost_estimate=pl.CostEstimate(flops=HEAD_FLOPS, bytes_accessed=1, transcendentals=0),
    )(order_of(rows, near_size, parts), *arrays)


def correlate(early, late, rows, groups, far, near_size, ch_dev):
    parts, inputs = 2 * ch_dev, groups * far * near_size * rows
    shape = (2, ch_dev, inputs, inputs)
    vmem, hbm = pl.BlockSpec(memory_space=pltpu.VMEM), pl.BlockSpec(memory_space=pltpu.HBM)
    return pl.pallas_call(
        functools.partial(gram_kernel, radix_of(ch_dev), ch_dev, rows, groups, far, near_size),
        out_shape=jax.ShapeDtypeStruct(shape, jnp.float32),
        in_specs=[vmem, hbm, vmem],
        out_specs=hbm,
        scratch_shapes=[
            pltpu.VMEM((parts, inputs, SPECTRA), jnp.bfloat16),
            pltpu.VMEM(shape, jnp.float32),
            pltpu.SemaphoreType.DMA((4,)),
            pltpu.SemaphoreType.DMA((ch_dev // GROUP,)),
        ],
        compiler_params=pltpu.CompilerParams(vmem_limit_bytes=TAIL_VMEM),
        cost_estimate=pl.CostEstimate(flops=1, bytes_accessed=1, transcendentals=0),
    )(order_of(rows, near_size, parts), pltpu.with_memory_space_constraint(early, pltpu.HBM), late)


def local(samples, taps):
    rows, count = samples.shape[:2]
    groups, far, near_size = lax.axis_size("grp"), lax.axis_size("far"), lax.axis_size("near")
    near = groups * near_size
    ch_dev = CHAN // (near * far)
    frames = samples.reshape(rows, count, TILES, LANES).transpose(1, 2, 0, 3).reshape(count, TILES * rows, LANES)
    table = jnp.asarray(tables(groups, far, near_size, ch_dev))
    sizes = (rows, groups, far, near_size, ch_dev)
    rest = SPECTRA // BLOCK - EARLY

    def cross(x, k):
        return lax.ppermute(x, "far", [(a, a ^ k) for a in range(far)])

    def swap(x, r):
        return lax.ppermute(x, ("grp", "near"), [(a, a ^ r) for a in range(near)])

    early = list(channelise(frames, taps, table, 0, 1, rows, groups, near_size, ch_dev, True))
    frames, early[0] = lax.optimization_barrier((frames, early[0]))
    (late,) = channelise(frames, taps, table, EARLY, rest, rows, groups, near_size, ch_dev, False)
    late = late.reshape(groups * far * near_size, *late.shape[3:])
    late = lax.all_to_all(late, ("grp", "far", "near"), split_axis=0, concat_axis=0, tiled=True)
    crossed = {k: cross(early[k], k) for k in range(far - 1, 0, -1)}
    crossed[0] = early[0]
    parcel = [jnp.stack([crossed[k][r] for k in range(far)], 0) for r in range(near)]
    first = parcel[:1] + [swap(parcel[r], r) for r in range(1, near)]
    return correlate(collect(first, *sizes), late, *sizes)


def solution(mesh):
    groups, members = mesh.shape["grp"], mesh.shape["dev"]
    finer = Mesh(mesh.devices.reshape(groups, members // 2, 2), ("grp", "far", "near"))
    whole = ("grp", "far", "near")
    return jax.shard_map(
        local,
        mesh=finer,
        in_specs=(P(whole, None, None), P()),
        out_specs=P(None, whole, None, None),
        check_vma=False,
    )
```

```python
import functools
import math

import jax
import jax.numpy as jnp
import numpy as np
from jax import lax
from jax.experimental import pallas as pl
from jax.experimental.pallas import tpu as pltpu
from jax.sharding import Mesh
from jax.sharding import PartitionSpec as P

BRANCH = 1024
CHAN = 512
TAPS = 4
SPECTRA = 512
GAIN = 2.0**-21
LANES = 128
TILES = BRANCH // LANES
ROWS = 8
BLOCK = 128
EARLY = 1
HEAD_FLOPS = 5 * 10**10
GROUP = 4
STEP = 8
PIECES = 2
HEAD_VMEM = 32 << 20
TAIL_VMEM = 32 << 20
FILTER_VMEM = 56 << 20

TERMS = {4: (((0, 0),), ((2, 1), (3, 2)), ((1, 3),), ((4, 1), (5, 2))), 1: (((0, 0),),)}


def radix_of(ch_dev):
    return 4 if 2 * ch_dev == 4 * ROWS else 1


def tables(groups, far, near, ch_dev):
    radix = radix_of(ch_dev)
    per = ch_dev // radix
    n = np.arange(BRANCH // radix)
    pieces = []
    for residue in (0, 2, 1, 3) if radix == 4 else (0,):
        chan = radix * np.arange(CHAN // radix).reshape(groups, far, near, per) + residue
        chan = chan.transpose(1, 0, 2, 3)[..., None]
        angle = 2.0 * math.pi / BRANCH * ((chan * n) % BRANCH)
        c, s = np.cos(angle), np.sin(angle)
        if residue == 1:
            pairs = [(c, -s), (-s, -c)]
        elif residue == 3:
            pairs = [(c, -s), (s, c)]
        else:
            pairs = [(c, -s)]
        for re, im in pairs:
            pieces.append(np.stack([re, im], 3).reshape(far, groups * near * 2 * per, -1))
    full = np.stack(pieces) * GAIN
    hi = full.astype(np.float32).astype(jnp.bfloat16)
    lo = (full - hi.astype(np.float64)).astype(np.float32).astype(jnp.bfloat16)
    return np.stack([hi, lo])


def split(x):
    hi = x.astype(jnp.bfloat16)
    return hi, (x - hi.astype(jnp.float32)).astype(jnp.bfloat16)


def product(w, f):
    return lax.dot_general(w, f, (((1,), (1,)), ((), ())), preferred_element_type=jnp.float32)


def filter_kernel(radix, rows, far, first, blocks, apart, x_ref, taps_ref, table_ref, *refs):
    outs, (f_ref, taps_f_ref, w_ref, held_ref, table_sem, x_sem) = refs[:-6], refs[-6:]
    wide = TILES * rows
    step = pl.program_id(0)
    slot = lax.rem(step, 2)
    size = BLOCK // PIECES
    table_copies = [
        pltpu.make_async_copy(table_ref.at[half, n], w_ref.at[half, n], table_sem.at[half, n])
        for n in range(w_ref.shape[1])
        for half in range(2)
    ]

    def fetch(step, slot, piece):
        low, high = (piece * size + TAPS - 1 if piece else 0), (piece + 1) * size + TAPS - 1
        return pltpu.make_async_copy(
            x_ref.at[pl.ds((first + step) * BLOCK + low, high - low)],
            held_ref.at[slot, low:high],
            x_sem.at[slot, piece],
        )

    @pl.when(step == 0)
    def _():
        for piece in range(PIECES):
            fetch(step, slot, piece).start()
        for copy in table_copies:
            copy.start()
        for t in range(TAPS):
            for h in range(TILES):
                tap = taps_ref[t : t + 1, h * LANES : (h + 1) * LANES].astype(jnp.float32)
                taps_f_ref[t, h * rows : (h + 1) * rows, :] = jnp.broadcast_to(tap, (rows, LANES))

    @pl.when(step + 1 < blocks)
    def _():
        for piece in range(PIECES):
            fetch(step + 1, 1 - slot, piece).start()

    def body(n, carry):
        at = pl.multiple_of(n * STEP, STEP)
        for h in range(0, wide, 8):
            x = held_ref[slot, pl.ds(at, STEP + TAPS - 1), h : h + 8, :].astype(jnp.float32)
            w = taps_f_ref[:, h : h + 8, :]
            f = w[0] * x[0:STEP]
            for t in range(1, TAPS):
                f = f + w[t] * x[t : t + STEP]
            f_ref[pl.ds(at, STEP), h : h + 8, :] = f
        return carry

    for piece in range(PIECES):
        fetch(step, slot, piece).wait()
        lax.fori_loop(piece * size // STEP, (piece + 1) * size // STEP, body, 0)

    @pl.when(step == 0)
    def _():
        for copy in table_copies:
            copy.wait()

    me_far, me_near = (lax.axis_index("far"), lax.axis_index(("grp", "near"))) if apart else (0, 0)
    stride = f_ref.shape[1]
    flat = f_ref.reshape(BLOCK * stride, LANES)
    tiles = TILES // radix

    def weights(half, piece):
        return jnp.concatenate([w_ref[half, piece, me_far ^ k] for k in range(far)], 0)

    for first in range(0, rows, 2):
        pair = (first, first + 1)

        def voltage(a):
            return jnp.concatenate(
                [
                    jnp.concatenate(
                        [flat[pl.ds((tiles * a + h) * rows + i, BLOCK, stride=stride), :] for h in range(tiles)], 1
                    )
                    for i in pair
                ],
                0,
            )

        if radix == 4:
            f0, f1, f2, f3 = (voltage(a) for a in range(4))
            even, odd = f0 + f2, f1 + f3
            ops = [split(even + odd), split(f0 - f2), split(f1 - f3), split(even - odd)]
        else:
            ops = [split(voltage(0))]
        sums = []
        for terms in TERMS[radix]:
            y = 0.0
            for piece, at in terms:
                hi, lo = ops[at]
                w_hi, w_lo = weights(0, piece), weights(1, piece)
                y = y + (product(w_hi, hi) + (product(w_hi, lo) + product(w_lo, hi)))
            sums.append(y)
        span = sums[0].shape[0] // far
        for k in range(far):
            for n, i in enumerate(pair):
                part = [
                    y[k * span : (k + 1) * span, n * BLOCK : (n + 1) * BLOCK].reshape(span // ROWS, ROWS, BLOCK)
                    for y in sums
                ]
                block = jnp.concatenate(part, 1).astype(jnp.bfloat16)
                if apart:
                    for p in range(block.shape[0]):
                        outs[k][me_near ^ p, i] = block[p]
                else:
                    groups, _, near_size = outs[0].shape[:3]
                    outs[0][:, k, :, 0, i] = block.reshape(groups, near_size, *block.shape[1:])


def channelise(frames, taps, table, first, blocks, rows, groups, near_size, ch_dev, apart):
    radix = radix_of(ch_dev)
    far = table.shape[2]
    near = groups * near_size
    parts = 2 * ch_dev
    wide = TILES * rows
    if apart:
        shape = (near, rows, parts, BLOCK)
        out_shape = [jax.ShapeDtypeStruct(shape, jnp.bfloat16)] * far
        out_specs = [pl.BlockSpec(shape, lambda j: (0, 0, 0, 0))] * far
    else:
        shape = (groups, far, near_size, blocks, rows, parts, BLOCK)
        out_shape = [jax.ShapeDtypeStruct(shape, jnp.bfloat16)]
        out_specs = [pl.BlockSpec(shape[:3] + (1,) + shape[4:], lambda j: (0, 0, 0, j, 0, 0, 0))]
    return pl.pallas_call(
        functools.partial(filter_kernel, radix, rows, far, first, blocks, apart),
        out_shape=out_shape,
        grid=(blocks,),
        in_specs=[
            pl.BlockSpec(memory_space=pltpu.HBM),
            pl.BlockSpec(taps.shape, lambda j: (0, 0)),
            pl.BlockSpec(memory_space=pltpu.HBM),
        ],
        out_specs=out_specs,
        scratch_shapes=[
            pltpu.VMEM((BLOCK, wide + 8, LANES), jnp.float32),
            pltpu.VMEM((TAPS, wide, LANES), jnp.float32),
            pltpu.VMEM(table.shape, table.dtype),
            pltpu.VMEM((2, BLOCK + TAPS - 1, wide, LANES), jnp.int32),
            pltpu.SemaphoreType.DMA(table.shape[:2]),
            pltpu.SemaphoreType.DMA((2, PIECES)),
        ],
        compiler_params=pltpu.CompilerParams(vmem_limit_bytes=FILTER_VMEM),
        cost_estimate=pl.CostEstimate(flops=1, bytes_accessed=1, transcendentals=0),
    )(frames, taps, table)


def turn(order, views, rows, parts, both):
    blocks = [jnp.concatenate([v[...].reshape(rows * parts, BLOCK) for v in near], 0) for near in views]
    y = jnp.dot(order, jnp.concatenate(blocks, 1), preferred_element_type=jnp.float32)
    return y.reshape(parts, both, len(views) * BLOCK)


def head_kernel(rows, groups, far, near_size, parts, order_ref, *refs):
    arrays, (o_ref, z_ref) = refs[:-2], refs[-2:]
    both = near_size * rows
    me_near, me_far = lax.axis_index(("grp", "near")), lax.axis_index("far")
    me_group, me_side = me_near // near_size, me_near % near_size
    order = order_ref[me_side]
    for g in range(groups):
        for k in range(far):
            at = (me_group ^ g) * far + (me_far ^ k)
            near = [arrays[g * near_size + x].at[k] for x in range(near_size)]
            z_ref[:, pl.ds(pl.multiple_of(at * both, both), both), :] = turn(order, [near], rows, parts, both)
    o_ref[...] = z_ref[...].astype(o_ref.dtype)


def gram_kernel(radix, ch_dev, rows, groups, far, near_size, order_ref, early_ref, late_ref, *refs):
    o_ref, z_ref, out_ref, early_sem, out_sem = refs
    parts = 2 * ch_dev
    both = near_size * rows
    pieces = early_sem.shape[0]
    size = parts // pieces
    fetches = []
    for n in range(pieces):
        part = pl.ds(n * size, size)
        fetches.append(pltpu.make_async_copy(early_ref.at[part], z_ref.at[part, :, 0:BLOCK], early_sem.at[n]))
        fetches[-1].start()
    order = order_ref[0]
    wide = 2 if far % 2 == 0 else 1
    for g in range(groups):
        for k in range(0, far, wide):
            turned = []
            for w in range(wide):
                at = (g * far + k + w) * near_size
                views = [
                    [late_ref.at[at + x, n] for x in range(near_size)] for n in range(late_ref.shape[1])
                ]
                turned.append(turn(order, views, rows, parts, both))
            low = (g * far + k) * both
            z_ref[:, low : low + wide * both, BLOCK:] = jnp.concatenate(turned, 1).astype(z_ref.dtype)
    for fetch in fetches:
        fetch.wait()
    inputs = z_ref.shape[1]
    per = ch_dev // radix
    copies = []
    for c in range(ch_dev):
        at = (c % radix) * 2 * per + c // radix
        z = jnp.concatenate([z_ref[at], z_ref[at + per]], 0)
        g = product(z, z)
        out_ref[0, c] = (g[:inputs, :inputs] + g[inputs:, inputs:]) * (1.0 / SPECTRA)
        out_ref[1, c] = (g[inputs:, :inputs] - g[:inputs, inputs:]) * (1.0 / SPECTRA)
        if (c + 1) % GROUP == 0:
            group = pl.ds(c + 1 - GROUP, GROUP)
            copies.append(
                pltpu.make_async_copy(out_ref.at[:, group], o_ref.at[:, group], out_sem.at[c // GROUP])
            )
            copies[-1].start()
    for copy in copies:
        copy.wait()


def order_of(rows, near_size, parts):
    both = near_size * rows
    wide = both * parts
    order = np.zeros((near_size, wide, wide), np.float32)
    for flip in range(near_size):
        for x in range(near_size):
            for i in range(rows):
                for b in range(parts):
                    order[flip, b * both + x * rows + i, ((x ^ flip) * rows + i) * parts + b] = 1.0
    return jnp.asarray(order, jnp.bfloat16)


def collect(arrays, rows, groups, far, near_size, ch_dev):
    parts, inputs = 2 * ch_dev, groups * far * near_size * rows
    vmem = pl.BlockSpec(memory_space=pltpu.VMEM)
    return pl.pallas_call(
        functools.partial(head_kernel, rows, groups, far, near_size, parts),
        out_shape=jax.ShapeDtypeStruct((parts, inputs, BLOCK), jnp.bfloat16),
        in_specs=[vmem] * (1 + len(arrays)),
        out_specs=vmem,
        scratch_shapes=[pltpu.VMEM((parts, inputs, BLOCK), jnp.float32)],
        compiler_params=pltpu.CompilerParams(vmem_limit_bytes=HEAD_VMEM),
        cost_estimate=pl.CostEstimate(flops=HEAD_FLOPS, bytes_accessed=1, transcendentals=0),
    )(order_of(rows, near_size, parts), *arrays)


def correlate(early, late, rows, groups, far, near_size, ch_dev):
    parts, inputs = 2 * ch_dev, groups * far * near_size * rows
    shape = (2, ch_dev, inputs, inputs)
    vmem, hbm = pl.BlockSpec(memory_space=pltpu.VMEM), pl.BlockSpec(memory_space=pltpu.HBM)
    return pl.pallas_call(
        functools.partial(gram_kernel, radix_of(ch_dev), ch_dev, rows, groups, far, near_size),
        out_shape=jax.ShapeDtypeStruct(shape, jnp.float32),
        in_specs=[vmem, hbm, vmem],
        out_specs=hbm,
        scratch_shapes=[
            pltpu.VMEM((parts, inputs, SPECTRA), jnp.bfloat16),
            pltpu.VMEM(shape, jnp.float32),
            pltpu.SemaphoreType.DMA((4,)),
            pltpu.SemaphoreType.DMA((ch_dev // GROUP,)),
        ],
        compiler_params=pltpu.CompilerParams(vmem_limit_bytes=TAIL_VMEM),
        cost_estimate=pl.CostEstimate(flops=1, bytes_accessed=1, transcendentals=0),
    )(order_of(rows, near_size, parts), pltpu.with_memory_space_constraint(early, pltpu.HBM), late)


def local(samples, taps):
    rows, count = samples.shape[:2]
    groups, far, near_size = lax.axis_size("grp"), lax.axis_size("far"), lax.axis_size("near")
    near = groups * near_size
    ch_dev = CHAN // (near * far)
    frames = samples.reshape(rows, count, TILES, LANES).transpose(1, 2, 0, 3).reshape(count, TILES * rows, LANES)
    table = jnp.asarray(tables(groups, far, near_size, ch_dev))
    sizes = (rows, groups, far, near_size, ch_dev)
    rest = SPECTRA // BLOCK - EARLY

    def cross(x, k):
        return lax.ppermute(x, "far", [(a, a ^ k) for a in range(far)])

    def swap(x, r):
        return lax.ppermute(x, ("grp", "near"), [(a, a ^ r) for a in range(near)])

    early = list(channelise(frames, taps, table, 0, 1, rows, groups, near_size, ch_dev, True))
    frames, early[0] = lax.optimization_barrier((frames, early[0]))
    (late,) = channelise(frames, taps, table, EARLY, rest, rows, groups, near_size, ch_dev, False)
    late = late.reshape(groups * far * near_size, *late.shape[3:])
    late = lax.all_to_all(late, ("grp", "far", "near"), split_axis=0, concat_axis=0, tiled=True)
    crossed = {k: cross(early[k], k) for k in range(far - 1, 0, -1)}
    crossed[0] = early[0]
    parcel = [jnp.stack([crossed[k][r] for k in range(far)], 0) for r in range(near)]
    first = parcel[:1] + [swap(parcel[r], r) for r in range(1, near)]
    return correlate(collect(first, *sizes), late, *sizes)


def solution(mesh):
    groups, members = mesh.shape["grp"], mesh.shape["dev"]
    finer = Mesh(mesh.devices.reshape(groups, members // 2, 2), ("grp", "far", "near"))
    whole = ("grp", "far", "near")
    return jax.shard_map(
        local,
        mesh=finer,
        in_specs=(P(whole, None, None), P()),
        out_specs=P(None, whole, None, None),
        check_vma=False,
    )
```

```python
import functools
import math

import jax
import jax.numpy as jnp
import numpy as np
from jax import lax
from jax.experimental import pallas as pl
from jax.experimental.pallas import tpu as pltpu
from jax.sharding import Mesh
from jax.sharding import PartitionSpec as P

BRANCH = 1024
CHAN = 512
TAPS = 4
SPECTRA = 512
GAIN = 2.0**-21
LANES = 128
TILES = BRANCH // LANES
ROWS = 8
BLOCK = 128
EARLY = 1
HEAD_FLOPS = 5 * 10**10
GROUP = 2
STEP = 8
PIECES = 2
HEAD_VMEM = 32 << 20
TAIL_VMEM = 32 << 20
FILTER_VMEM = 56 << 20

TERMS = {4: (((0, 0),), ((2, 1), (3, 2)), ((1, 3),), ((4, 1), (5, 2))), 1: (((0, 0),),)}


def radix_of(ch_dev):
    return 4 if 2 * ch_dev == 4 * ROWS else 1


def tables(groups, far, near, ch_dev):
    radix = radix_of(ch_dev)
    per = ch_dev // radix
    n = np.arange(BRANCH // radix)
    pieces = []
    for residue in (0, 2, 1, 3) if radix == 4 else (0,):
        chan = radix * np.arange(CHAN // radix).reshape(groups, far, near, per) + residue
        chan = chan.transpose(1, 0, 2, 3)[..., None]
        angle = 2.0 * math.pi / BRANCH * ((chan * n) % BRANCH)
        c, s = np.cos(angle), np.sin(angle)
        if residue == 1:
            pairs = [(c, -s), (-s, -c)]
        elif residue == 3:
            pairs = [(c, -s), (s, c)]
        else:
            pairs = [(c, -s)]
        for re, im in pairs:
            pieces.append(np.stack([re, im], 3).reshape(far, groups * near * 2 * per, -1))
    full = np.stack(pieces) * GAIN
    hi = full.astype(np.float32).astype(jnp.bfloat16)
    lo = (full - hi.astype(np.float64)).astype(np.float32).astype(jnp.bfloat16)
    return np.stack([hi, lo])


def split(x):
    hi = x.astype(jnp.bfloat16)
    return hi, (x - hi.astype(jnp.float32)).astype(jnp.bfloat16)


def product(w, f):
    return lax.dot_general(w, f, (((1,), (1,)), ((), ())), preferred_element_type=jnp.float32)


def filter_kernel(radix, rows, far, first, blocks, apart, x_ref, taps_ref, table_ref, *refs):
    outs, (f_ref, taps_f_ref, w_ref, held_ref, table_sem, x_sem) = refs[:-6], refs[-6:]
    wide = TILES * rows
    step = pl.program_id(0)
    slot = lax.rem(step, 2)
    size = BLOCK // PIECES
    table_copies = [
        pltpu.make_async_copy(table_ref.at[half, n], w_ref.at[half, n], table_sem.at[half, n])
        for n in range(w_ref.shape[1])
        for half in range(2)
    ]

    def fetch(step, slot, piece):
        low, high = (piece * size + TAPS - 1 if piece else 0), (piece + 1) * size + TAPS - 1
        return pltpu.make_async_copy(
            x_ref.at[pl.ds((first + step) * BLOCK + low, high - low)],
            held_ref.at[slot, low:high],
            x_sem.at[slot, piece],
        )

    @pl.when(step == 0)
    def _():
        for piece in range(PIECES):
            fetch(step, slot, piece).start()
        for copy in table_copies:
            copy.start()
        for t in range(TAPS):
            for h in range(TILES):
                tap = taps_ref[t : t + 1, h * LANES : (h + 1) * LANES].astype(jnp.float32)
                taps_f_ref[t, h * rows : (h + 1) * rows, :] = jnp.broadcast_to(tap, (rows, LANES))

    @pl.when(step + 1 < blocks)
    def _():
        for piece in range(PIECES):
            fetch(step + 1, 1 - slot, piece).start()

    def body(n, carry):
        at = pl.multiple_of(n * STEP, STEP)
        for h in range(0, wide, 8):
            x = held_ref[slot, pl.ds(at, STEP + TAPS - 1), h : h + 8, :].astype(jnp.float32)
            w = taps_f_ref[:, h : h + 8, :]
            f = w[0] * x[0:STEP]
            for t in range(1, TAPS):
                f = f + w[t] * x[t : t + STEP]
            f_ref[pl.ds(at, STEP), h : h + 8, :] = f
        return carry

    for piece in range(PIECES):
        fetch(step, slot, piece).wait()
        lax.fori_loop(piece * size // STEP, (piece + 1) * size // STEP, body, 0)

    @pl.when(step == 0)
    def _():
        for copy in table_copies:
            copy.wait()

    me_far, me_near = (lax.axis_index("far"), lax.axis_index(("grp", "near"))) if apart else (0, 0)
    stride = f_ref.shape[1]
    flat = f_ref.reshape(BLOCK * stride, LANES)
    tiles = TILES // radix

    def weights(half, piece):
        return jnp.concatenate([w_ref[half, piece, me_far ^ k] for k in range(far)], 0)

    for first in range(0, rows, 2):
        pair = (first, first + 1)

        def voltage(a):
            return jnp.concatenate(
                [
                    jnp.concatenate(
                        [flat[pl.ds((tiles * a + h) * rows + i, BLOCK, stride=stride), :] for h in range(tiles)], 1
                    )
                    for i in pair
                ],
                0,
            )

        if radix == 4:
            f0, f1, f2, f3 = (voltage(a) for a in range(4))
            even, odd = f0 + f2, f1 + f3
            ops = [split(even + odd), split(f0 - f2), split(f1 - f3), split(even - odd)]
        else:
            ops = [split(voltage(0))]
        sums = []
        for terms in TERMS[radix]:
            y = 0.0
            for piece, at in terms:
                hi, lo = ops[at]
                w_hi, w_lo = weights(0, piece), weights(1, piece)
                y = y + (product(w_hi, hi) + (product(w_hi, lo) + product(w_lo, hi)))
            sums.append(y)
        span = sums[0].shape[0] // far
        for k in range(far):
            for n, i in enumerate(pair):
                part = [
                    y[k * span : (k + 1) * span, n * BLOCK : (n + 1) * BLOCK].reshape(span // ROWS, ROWS, BLOCK)
                    for y in sums
                ]
                block = jnp.concatenate(part, 1).astype(jnp.bfloat16)
                if apart:
                    for p in range(block.shape[0]):
                        outs[k][me_near ^ p, i] = block[p]
                else:
                    groups, _, near_size = outs[0].shape[:3]
                    outs[0][:, k, :, 0, i] = block.reshape(groups, near_size, *block.shape[1:])


def channelise(frames, taps, table, first, blocks, rows, groups, near_size, ch_dev, apart):
    radix = radix_of(ch_dev)
    far = table.shape[2]
    near = groups * near_size
    parts = 2 * ch_dev
    wide = TILES * rows
    if apart:
        shape = (near, rows, parts, BLOCK)
        out_shape = [jax.ShapeDtypeStruct(shape, jnp.bfloat16)] * far
        out_specs = [pl.BlockSpec(shape, lambda j: (0, 0, 0, 0))] * far
    else:
        shape = (groups, far, near_size, blocks, rows, parts, BLOCK)
        out_shape = [jax.ShapeDtypeStruct(shape, jnp.bfloat16)]
        out_specs = [pl.BlockSpec(shape[:3] + (1,) + shape[4:], lambda j: (0, 0, 0, j, 0, 0, 0))]
    return pl.pallas_call(
        functools.partial(filter_kernel, radix, rows, far, first, blocks, apart),
        out_shape=out_shape,
        grid=(blocks,),
        in_specs=[
            pl.BlockSpec(memory_space=pltpu.HBM),
            pl.BlockSpec(taps.shape, lambda j: (0, 0)),
            pl.BlockSpec(memory_space=pltpu.HBM),
        ],
        out_specs=out_specs,
        scratch_shapes=[
            pltpu.VMEM((BLOCK, wide + 8, LANES), jnp.float32),
            pltpu.VMEM((TAPS, wide, LANES), jnp.float32),
            pltpu.VMEM(table.shape, table.dtype),
            pltpu.VMEM((2, BLOCK + TAPS - 1, wide, LANES), jnp.int32),
            pltpu.SemaphoreType.DMA(table.shape[:2]),
            pltpu.SemaphoreType.DMA((2, PIECES)),
        ],
        compiler_params=pltpu.CompilerParams(vmem_limit_bytes=FILTER_VMEM),
        cost_estimate=pl.CostEstimate(flops=1, bytes_accessed=1, transcendentals=0),
    )(frames, taps, table)


def turn(order, views, rows, parts, both):
    blocks = [jnp.concatenate([v[...].reshape(rows * parts, BLOCK) for v in near], 0) for near in views]
    y = jnp.dot(order, jnp.concatenate(blocks, 1), preferred_element_type=jnp.float32)
    return y.reshape(parts, both, len(views) * BLOCK)


def head_kernel(rows, groups, far, near_size, parts, order_ref, *refs):
    arrays, (o_ref, z_ref) = refs[:-2], refs[-2:]
    both = near_size * rows
    me_near, me_far = lax.axis_index(("grp", "near")), lax.axis_index("far")
    me_group, me_side = me_near // near_size, me_near % near_size
    order = order_ref[me_side]
    for g in range(groups):
        for k in range(far):
            at = (me_group ^ g) * far + (me_far ^ k)
            near = [arrays[g * near_size + x].at[k] for x in range(near_size)]
            z_ref[:, pl.ds(pl.multiple_of(at * both, both), both), :] = turn(order, [near], rows, parts, both)
    o_ref[...] = z_ref[...].astype(o_ref.dtype)


def gram_kernel(radix, ch_dev, rows, groups, far, near_size, order_ref, early_ref, late_ref, *refs):
    o_ref, z_ref, out_ref, early_sem, out_sem = refs
    parts = 2 * ch_dev
    both = near_size * rows
    pieces = early_sem.shape[0]
    size = parts // pieces
    fetches = []
    for n in range(pieces):
        part = pl.ds(n * size, size)
        fetches.append(pltpu.make_async_copy(early_ref.at[part], z_ref.at[part, :, 0:BLOCK], early_sem.at[n]))
        fetches[-1].start()
    order = order_ref[0]
    wide = 2 if far % 2 == 0 else 1
    for g in range(groups):
        for k in range(0, far, wide):
            turned = []
            for w in range(wide):
                at = (g * far + k + w) * near_size
                views = [
                    [late_ref.at[at + x, n] for x in range(near_size)] for n in range(late_ref.shape[1])
                ]
                turned.append(turn(order, views, rows, parts, both))
            low = (g * far + k) * both
            z_ref[:, low : low + wide * both, BLOCK:] = jnp.concatenate(turned, 1).astype(z_ref.dtype)
    for fetch in fetches:
        fetch.wait()
    inputs = z_ref.shape[1]
    per = ch_dev // radix
    copies = []
    for c in range(ch_dev):
        at = (c % radix) * 2 * per + c // radix
        z = jnp.concatenate([z_ref[at], z_ref[at + per]], 0)
        g = product(z, z)
        out_ref[0, c] = (g[:inputs, :inputs] + g[inputs:, inputs:]) * (1.0 / SPECTRA)
        out_ref[1, c] = (g[inputs:, :inputs] - g[:inputs, inputs:]) * (1.0 / SPECTRA)
        if (c + 1) % GROUP == 0:
            group = pl.ds(c + 1 - GROUP, GROUP)
            copies.append(
                pltpu.make_async_copy(out_ref.at[:, group], o_ref.at[:, group], out_sem.at[c // GROUP])
            )
            copies[-1].start()
    for copy in copies:
        copy.wait()


def order_of(rows, near_size, parts):
    both = near_size * rows
    wide = both * parts
    order = np.zeros((near_size, wide, wide), np.float32)
    for flip in range(near_size):
        for x in range(near_size):
            for i in range(rows):
                for b in range(parts):
                    order[flip, b * both + x * rows + i, ((x ^ flip) * rows + i) * parts + b] = 1.0
    return jnp.asarray(order, jnp.bfloat16)


def collect(arrays, rows, groups, far, near_size, ch_dev):
    parts, inputs = 2 * ch_dev, groups * far * near_size * rows
    vmem = pl.BlockSpec(memory_space=pltpu.VMEM)
    return pl.pallas_call(
        functools.partial(head_kernel, rows, groups, far, near_size, parts),
        out_shape=jax.ShapeDtypeStruct((parts, inputs, BLOCK), jnp.bfloat16),
        in_specs=[vmem] * (1 + len(arrays)),
        out_specs=vmem,
        scratch_shapes=[pltpu.VMEM((parts, inputs, BLOCK), jnp.float32)],
        compiler_params=pltpu.CompilerParams(vmem_limit_bytes=HEAD_VMEM),
        cost_estimate=pl.CostEstimate(flops=HEAD_FLOPS, bytes_accessed=1, transcendentals=0),
    )(order_of(rows, near_size, parts), *arrays)


def correlate(early, late, rows, groups, far, near_size, ch_dev):
    parts, inputs = 2 * ch_dev, groups * far * near_size * rows
    shape = (2, ch_dev, inputs, inputs)
    vmem, hbm = pl.BlockSpec(memory_space=pltpu.VMEM), pl.BlockSpec(memory_space=pltpu.HBM)
    return pl.pallas_call(
        functools.partial(gram_kernel, radix_of(ch_dev), ch_dev, rows, groups, far, near_size),
        out_shape=jax.ShapeDtypeStruct(shape, jnp.float32),
        in_specs=[vmem, hbm, vmem],
        out_specs=hbm,
        scratch_shapes=[
            pltpu.VMEM((parts, inputs, SPECTRA), jnp.bfloat16),
            pltpu.VMEM(shape, jnp.float32),
            pltpu.SemaphoreType.DMA((4,)),
            pltpu.SemaphoreType.DMA((ch_dev // GROUP,)),
        ],
        compiler_params=pltpu.CompilerParams(vmem_limit_bytes=TAIL_VMEM),
        cost_estimate=pl.CostEstimate(flops=1, bytes_accessed=1, transcendentals=0),
    )(order_of(rows, near_size, parts), pltpu.with_memory_space_constraint(early, pltpu.HBM), late)


def local(samples, taps):
    rows, count = samples.shape[:2]
    groups, far, near_size = lax.axis_size("grp"), lax.axis_size("far"), lax.axis_size("near")
    near = groups * near_size
    ch_dev = CHAN // (near * far)
    frames = samples.reshape(rows, count, TILES, LANES).transpose(1, 2, 0, 3).reshape(count, TILES * rows, LANES)
    table = jnp.asarray(tables(groups, far, near_size, ch_dev))
    sizes = (rows, groups, far, near_size, ch_dev)
    rest = SPECTRA // BLOCK - EARLY

    def cross(x, k):
        return lax.ppermute(x, "far", [(a, a ^ k) for a in range(far)])

    def swap(x, r):
        return lax.ppermute(x, ("grp", "near"), [(a, a ^ r) for a in range(near)])

    early = list(channelise(frames, taps, table, 0, 1, rows, groups, near_size, ch_dev, True))
    frames, early[0] = lax.optimization_barrier((frames, early[0]))
    (late,) = channelise(frames, taps, table, EARLY, rest, rows, groups, near_size, ch_dev, False)
    late = late.reshape(groups * far * near_size, *late.shape[3:])
    late = lax.all_to_all(late, ("grp", "far", "near"), split_axis=0, concat_axis=0, tiled=True)
    crossed = {k: cross(early[k], k) for k in range(far - 1, 0, -1)}
    crossed[0] = early[0]
    parcel = [jnp.stack([crossed[k][r] for k in range(far)], 0) for r in range(near)]
    first = parcel[:1] + [swap(parcel[r], r) for r in range(1, near)]
    return correlate(collect(first, *sizes), late, *sizes)


def solution(mesh):
    groups, members = mesh.shape["grp"], mesh.shape["dev"]
    finer = Mesh(mesh.devices.reshape(groups, members // 2, 2), ("grp", "far", "near"))
    whole = ("grp", "far", "near")
    return jax.shard_map(
        local,
        mesh=finer,
        in_specs=(P(whole, None, None), P()),
        out_specs=P(None, whole, None, None),
        check_vma=False,
    )
```

```python
import functools
import math

import jax
import jax.numpy as jnp
import numpy as np
from jax import lax
from jax.experimental import pallas as pl
from jax.experimental.pallas import tpu as pltpu
from jax.sharding import Mesh
from jax.sharding import PartitionSpec as P

BRANCH = 1024
CHAN = 512
TAPS = 4
SPECTRA = 512
GAIN = 2.0**-21
LANES = 128
TILES = BRANCH // LANES
ROWS = 8
BLOCK = 128
EARLY = 1
HEAD_FLOPS = 5 * 10**10
GROUP = 2
STEP = 16
PIECES = 2
HEAD_VMEM = 32 << 20
TAIL_VMEM = 32 << 20
FILTER_VMEM = 56 << 20

TERMS = {4: (((0, 0),), ((2, 1), (3, 2)), ((1, 3),), ((4, 1), (5, 2))), 1: (((0, 0),),)}


def radix_of(ch_dev):
    return 4 if 2 * ch_dev == 4 * ROWS else 1


def tables(groups, far, near, ch_dev):
    radix = radix_of(ch_dev)
    per = ch_dev // radix
    n = np.arange(BRANCH // radix)
    pieces = []
    for residue in (0, 2, 1, 3) if radix == 4 else (0,):
        chan = radix * np.arange(CHAN // radix).reshape(groups, far, near, per) + residue
        chan = chan.transpose(1, 0, 2, 3)[..., None]
        angle = 2.0 * math.pi / BRANCH * ((chan * n) % BRANCH)
        c, s = np.cos(angle), np.sin(angle)
        if residue == 1:
            pairs = [(c, -s), (-s, -c)]
        elif residue == 3:
            pairs = [(c, -s), (s, c)]
        else:
            pairs = [(c, -s)]
        for re, im in pairs:
            pieces.append(np.stack([re, im], 3).reshape(far, groups * near * 2 * per, -1))
    full = np.stack(pieces) * GAIN
    hi = full.astype(np.float32).astype(jnp.bfloat16)
    lo = (full - hi.astype(np.float64)).astype(np.float32).astype(jnp.bfloat16)
    return np.stack([hi, lo])


def split(x):
    hi = x.astype(jnp.bfloat16)
    return hi, (x - hi.astype(jnp.float32)).astype(jnp.bfloat16)


def product(w, f):
    return lax.dot_general(w, f, (((1,), (1,)), ((), ())), preferred_element_type=jnp.float32)


def filter_kernel(radix, rows, far, first, blocks, apart, x_ref, taps_ref, table_ref, *refs):
    outs, (f_ref, taps_f_ref, w_ref, held_ref, table_sem, x_sem) = refs[:-6], refs[-6:]
    wide = TILES * rows
    step = pl.program_id(0)
    slot = lax.rem(step, 2)
    size = BLOCK // PIECES
    table_copies = [
        pltpu.make_async_copy(table_ref.at[half, n], w_ref.at[half, n], table_sem.at[half, n])
        for n in range(w_ref.shape[1])
        for half in range(2)
    ]

    def fetch(step, slot, piece):
        low, high = (piece * size + TAPS - 1 if piece else 0), (piece + 1) * size + TAPS - 1
        return pltpu.make_async_copy(
            x_ref.at[pl.ds((first + step) * BLOCK + low, high - low)],
            held_ref.at[slot, low:high],
            x_sem.at[slot, piece],
        )

    @pl.when(step == 0)
    def _():
        for piece in range(PIECES):
            fetch(step, slot, piece).start()
        for copy in table_copies:
            copy.start()
        for t in range(TAPS):
            for h in range(TILES):
                tap = taps_ref[t : t + 1, h * LANES : (h + 1) * LANES].astype(jnp.float32)
                taps_f_ref[t, h * rows : (h + 1) * rows, :] = jnp.broadcast_to(tap, (rows, LANES))

    @pl.when(step + 1 < blocks)
    def _():
        for piece in range(PIECES):
            fetch(step + 1, 1 - slot, piece).start()

    def body(n, carry):
        at = pl.multiple_of(n * STEP, STEP)
        for h in range(0, wide, 8):
            x = held_ref[slot, pl.ds(at, STEP + TAPS - 1), h : h + 8, :].astype(jnp.float32)
            w = taps_f_ref[:, h : h + 8, :]
            f = w[0] * x[0:STEP]
            for t in range(1, TAPS):
                f = f + w[t] * x[t : t + STEP]
            f_ref[pl.ds(at, STEP), h : h + 8, :] = f
        return carry

    for piece in range(PIECES):
        fetch(step, slot, piece).wait()
        lax.fori_loop(piece * size // STEP, (piece + 1) * size // STEP, body, 0)

    @pl.when(step == 0)
    def _():
        for copy in table_copies:
            copy.wait()

    me_far, me_near = (lax.axis_index("far"), lax.axis_index(("grp", "near"))) if apart else (0, 0)
    stride = f_ref.shape[1]
    flat = f_ref.reshape(BLOCK * stride, LANES)
    tiles = TILES // radix

    def weights(half, piece):
        return jnp.concatenate([w_ref[half, piece, me_far ^ k] for k in range(far)], 0)

    for first in range(0, rows, 2):
        pair = (first, first + 1)

        def voltage(a):
            return jnp.concatenate(
                [
                    jnp.concatenate(
                        [flat[pl.ds((tiles * a + h) * rows + i, BLOCK, stride=stride), :] for h in range(tiles)], 1
                    )
                    for i in pair
                ],
                0,
            )

        if radix == 4:
            f0, f1, f2, f3 = (voltage(a) for a in range(4))
            even, odd = f0 + f2, f1 + f3
            ops = [split(even + odd), split(f0 - f2), split(f1 - f3), split(even - odd)]
        else:
            ops = [split(voltage(0))]
        sums = []
        for terms in TERMS[radix]:
            y = 0.0
            for piece, at in terms:
                hi, lo = ops[at]
                w_hi, w_lo = weights(0, piece), weights(1, piece)
                y = y + (product(w_hi, hi) + (product(w_hi, lo) + product(w_lo, hi)))
            sums.append(y)
        span = sums[0].shape[0] // far
        for k in range(far):
            for n, i in enumerate(pair):
                part = [
                    y[k * span : (k + 1) * span, n * BLOCK : (n + 1) * BLOCK].reshape(span // ROWS, ROWS, BLOCK)
                    for y in sums
                ]
                block = jnp.concatenate(part, 1).astype(jnp.bfloat16)
                if apart:
                    for p in range(block.shape[0]):
                        outs[k][me_near ^ p, i] = block[p]
                else:
                    groups, _, near_size = outs[0].shape[:3]
                    outs[0][:, k, :, 0, i] = block.reshape(groups, near_size, *block.shape[1:])


def channelise(frames, taps, table, first, blocks, rows, groups, near_size, ch_dev, apart):
    radix = radix_of(ch_dev)
    far = table.shape[2]
    near = groups * near_size
    parts = 2 * ch_dev
    wide = TILES * rows
    if apart:
        shape = (near, rows, parts, BLOCK)
        out_shape = [jax.ShapeDtypeStruct(shape, jnp.bfloat16)] * far
        out_specs = [pl.BlockSpec(shape, lambda j: (0, 0, 0, 0))] * far
    else:
        shape = (groups, far, near_size, blocks, rows, parts, BLOCK)
        out_shape = [jax.ShapeDtypeStruct(shape, jnp.bfloat16)]
        out_specs = [pl.BlockSpec(shape[:3] + (1,) + shape[4:], lambda j: (0, 0, 0, j, 0, 0, 0))]
    return pl.pallas_call(
        functools.partial(filter_kernel, radix, rows, far, first, blocks, apart),
        out_shape=out_shape,
        grid=(blocks,),
        in_specs=[
            pl.BlockSpec(memory_space=pltpu.HBM),
            pl.BlockSpec(taps.shape, lambda j: (0, 0)),
            pl.BlockSpec(memory_space=pltpu.HBM),
        ],
        out_specs=out_specs,
        scratch_shapes=[
            pltpu.VMEM((BLOCK, wide + 8, LANES), jnp.float32),
            pltpu.VMEM((TAPS, wide, LANES), jnp.float32),
            pltpu.VMEM(table.shape, table.dtype),
            pltpu.VMEM((2, BLOCK + TAPS - 1, wide, LANES), jnp.int32),
            pltpu.SemaphoreType.DMA(table.shape[:2]),
            pltpu.SemaphoreType.DMA((2, PIECES)),
        ],
        compiler_params=pltpu.CompilerParams(vmem_limit_bytes=FILTER_VMEM),
        cost_estimate=pl.CostEstimate(flops=1, bytes_accessed=1, transcendentals=0),
    )(frames, taps, table)


def turn(order, views, rows, parts, both):
    blocks = [jnp.concatenate([v[...].reshape(rows * parts, BLOCK) for v in near], 0) for near in views]
    y = jnp.dot(order, jnp.concatenate(blocks, 1), preferred_element_type=jnp.float32)
    return y.reshape(parts, both, len(views) * BLOCK)


def head_kernel(rows, groups, far, near_size, parts, order_ref, *refs):
    arrays, (o_ref, z_ref) = refs[:-2], refs[-2:]
    both = near_size * rows
    me_near, me_far = lax.axis_index(("grp", "near")), lax.axis_index("far")
    me_group, me_side = me_near // near_size, me_near % near_size
    order = order_ref[me_side]
    for g in range(groups):
        for k in range(far):
            at = (me_group ^ g) * far + (me_far ^ k)
            near = [arrays[g * near_size + x].at[k] for x in range(near_size)]
            z_ref[:, pl.ds(pl.multiple_of(at * both, both), both), :] = turn(order, [near], rows, parts, both)
    o_ref[...] = z_ref[...].astype(o_ref.dtype)


def gram_kernel(radix, ch_dev, rows, groups, far, near_size, order_ref, early_ref, late_ref, *refs):
    o_ref, z_ref, out_ref, early_sem, out_sem = refs
    parts = 2 * ch_dev
    both = near_size * rows
    pieces = early_sem.shape[0]
    size = parts // pieces
    fetches = []
    for n in range(pieces):
        part = pl.ds(n * size, size)
        fetches.append(pltpu.make_async_copy(early_ref.at[part], z_ref.at[part, :, 0:BLOCK], early_sem.at[n]))
        fetches[-1].start()
    order = order_ref[0]
    wide = 2 if far % 2 == 0 else 1
    for g in range(groups):
        for k in range(0, far, wide):
            turned = []
            for w in range(wide):
                at = (g * far + k + w) * near_size
                views = [
                    [late_ref.at[at + x, n] for x in range(near_size)] for n in range(late_ref.shape[1])
                ]
                turned.append(turn(order, views, rows, parts, both))
            low = (g * far + k) * both
            z_ref[:, low : low + wide * both, BLOCK:] = jnp.concatenate(turned, 1).astype(z_ref.dtype)
    for fetch in fetches:
        fetch.wait()
    inputs = z_ref.shape[1]
    per = ch_dev // radix
    copies = []
    for c in range(ch_dev):
        at = (c % radix) * 2 * per + c // radix
        z = jnp.concatenate([z_ref[at], z_ref[at + per]], 0)
        g = product(z, z)
        out_ref[0, c] = (g[:inputs, :inputs] + g[inputs:, inputs:]) * (1.0 / SPECTRA)
        out_ref[1, c] = (g[inputs:, :inputs] - g[:inputs, inputs:]) * (1.0 / SPECTRA)
        if (c + 1) % GROUP == 0:
            group = pl.ds(c + 1 - GROUP, GROUP)
            copies.append(
                pltpu.make_async_copy(out_ref.at[:, group], o_ref.at[:, group], out_sem.at[c // GROUP])
            )
            copies[-1].start()
    for copy in copies:
        copy.wait()


def order_of(rows, near_size, parts):
    both = near_size * rows
    wide = both * parts
    order = np.zeros((near_size, wide, wide), np.float32)
    for flip in range(near_size):
        for x in range(near_size):
            for i in range(rows):
                for b in range(parts):
                    order[flip, b * both + x * rows + i, ((x ^ flip) * rows + i) * parts + b] = 1.0
    return jnp.asarray(order, jnp.bfloat16)


def collect(arrays, rows, groups, far, near_size, ch_dev):
    parts, inputs = 2 * ch_dev, groups * far * near_size * rows
    vmem = pl.BlockSpec(memory_space=pltpu.VMEM)
    return pl.pallas_call(
        functools.partial(head_kernel, rows, groups, far, near_size, parts),
        out_shape=jax.ShapeDtypeStruct((parts, inputs, BLOCK), jnp.bfloat16),
        in_specs=[vmem] * (1 + len(arrays)),
        out_specs=vmem,
        scratch_shapes=[pltpu.VMEM((parts, inputs, BLOCK), jnp.float32)],
        compiler_params=pltpu.CompilerParams(vmem_limit_bytes=HEAD_VMEM),
        cost_estimate=pl.CostEstimate(flops=HEAD_FLOPS, bytes_accessed=1, transcendentals=0),
    )(order_of(rows, near_size, parts), *arrays)


def correlate(early, late, rows, groups, far, near_size, ch_dev):
    parts, inputs = 2 * ch_dev, groups * far * near_size * rows
    shape = (2, ch_dev, inputs, inputs)
    vmem, hbm = pl.BlockSpec(memory_space=pltpu.VMEM), pl.BlockSpec(memory_space=pltpu.HBM)
    return pl.pallas_call(
        functools.partial(gram_kernel, radix_of(ch_dev), ch_dev, rows, groups, far, near_size),
        out_shape=jax.ShapeDtypeStruct(shape, jnp.float32),
        in_specs=[vmem, hbm, vmem],
        out_specs=hbm,
        scratch_shapes=[
            pltpu.VMEM((parts, inputs, SPECTRA), jnp.bfloat16),
            pltpu.VMEM(shape, jnp.float32),
            pltpu.SemaphoreType.DMA((4,)),
            pltpu.SemaphoreType.DMA((ch_dev // GROUP,)),
        ],
        compiler_params=pltpu.CompilerParams(vmem_limit_bytes=TAIL_VMEM),
        cost_estimate=pl.CostEstimate(flops=1, bytes_accessed=1, transcendentals=0),
    )(order_of(rows, near_size, parts), pltpu.with_memory_space_constraint(early, pltpu.HBM), late)


def local(samples, taps):
    rows, count = samples.shape[:2]
    groups, far, near_size = lax.axis_size("grp"), lax.axis_size("far"), lax.axis_size("near")
    near = groups * near_size
    ch_dev = CHAN // (near * far)
    frames = samples.reshape(rows, count, TILES, LANES).transpose(1, 2, 0, 3).reshape(count, TILES * rows, LANES)
    table = jnp.asarray(tables(groups, far, near_size, ch_dev))
    sizes = (rows, groups, far, near_size, ch_dev)
    rest = SPECTRA // BLOCK - EARLY

    def cross(x, k):
        return lax.ppermute(x, "far", [(a, a ^ k) for a in range(far)])

    def swap(x, r):
        return lax.ppermute(x, ("grp", "near"), [(a, a ^ r) for a in range(near)])

    early = list(channelise(frames, taps, table, 0, 1, rows, groups, near_size, ch_dev, True))
    frames, early[0] = lax.optimization_barrier((frames, early[0]))
    (late,) = channelise(frames, taps, table, EARLY, rest, rows, groups, near_size, ch_dev, False)
    late = late.reshape(groups * far * near_size, *late.shape[3:])
    late = lax.all_to_all(late, ("grp", "far", "near"), split_axis=0, concat_axis=0, tiled=True)
    crossed = {k: cross(early[k], k) for k in range(far - 1, 0, -1)}
    crossed[0] = early[0]
    parcel = [jnp.stack([crossed[k][r] for k in range(far)], 0) for r in range(near)]
    first = parcel[:1] + [swap(parcel[r], r) for r in range(1, near)]
    return correlate(collect(first, *sizes), late, *sizes)


def solution(mesh):
    groups, members = mesh.shape["grp"], mesh.shape["dev"]
    finer = Mesh(mesh.devices.reshape(groups, members // 2, 2), ("grp", "far", "near"))
    whole = ("grp", "far", "near")
    return jax.shard_map(
        local,
        mesh=finer,
        in_specs=(P(whole, None, None), P()),
        out_specs=P(None, whole, None, None),
        check_vma=False,
    )
```
